32 devices in a mesh: dom: 8 (over z, y), sub: 4 (over x, core).
Axes of the slice: x: 2, y: 2, z: 4, core: 2. Of those that a mesh axis runs over, the one named last changes fastest.
Arguments:
- velocity: float32 [5, 262144], P(None, ('dom', 'sub')), may hold values from -6 to 6
- position: float32 [3, 262144], P(None, ('dom', 'sub')), may hold values from 0 to 1
- inv_mass: float32 [262144], P(('dom', 'sub')), may hold values from 0.05 to 0.3
- connectivity: int32 [4, 262144], P(None, ('dom', 'sub')), may hold values from 0 to 8447, as said below
- shape_grad: float32 [2, 4, 262144], P(None, None, ('dom', 'sub')), may hold values from -3 to 3
- area: float32 [262144], P(('dom', 'sub')), may hold values from 0.5 to 2
- thickness: float32 [262144], P(('dom', 'sub')), may hold values from 0.5 to 1.5
- yield_stress: float32 [262144], P(('dom', 'sub')), may hold values from 0.5 to 3
- stress: float32 [5, 5, 262144], P(None, None, ('dom', 'sub')), may hold values from -6 to 6
- contact_owner: int32 [262144, 1], P(('dom', 'sub')), may hold values from 0 to 31; in each aligned block of 8192 rows (0 to 8191, 8192 to 16383, ...) at most 512 rows name the same one
- face_center: float32 [3, 65536], P(None, ('dom', 'sub')), may hold values from 0 to 1
- face_angle: float32 [2, 65536], P(None, ('dom', 'sub')), may hold values from -3.140625 to 3.140625
- face_stiffness: float32 [65536], P(('dom', 'sub')), may hold values from 1 to 10
- ghost_list: int32 [16384], P(('dom', 'sub')), may hold values from 0 to 2047
- pair_node: int32 [4096], P(('dom', 'sub')), may hold values from 0 to 127
- pair_face: int32 [4096], P(('dom', 'sub')), may hold values from 0 to 19
- pair_count: int32 [32], P(('dom', 'sub')), may hold values from 16 to 128, as said below
Outputs:
- new_velocity: float32 [5, 262144], P(None, ('dom', 'sub'))
- new_stress: float32 [5, 5, 262144], P(None, None, ('dom', 'sub'))
The draws below stay inside these ranges and needn't reach their ends.
Inputs may be any that keep to these rules, and one draw needn't show every extreme that they name: `connectivity`: the corners of the element at local index e of a device lie in e .. e + 256; on the first device at least 128, on the last below 8320. `contact_owner`: the 8192 nodes of one device name any one contact device at most 512 times; some device reaches 512. `pair_count`: some device's count is 128 in every draw.
All inputs are finite; a program needn't handle non-finite values.
Results may differ from the reference program's by a relative error of at most 0.0003.
Values sent between devices are 32-bit elements; how exact they have to be, the bound alone decides.
No kernel may reach another device: no remote copies, remote signals or barrier semaphores. Data moves between devices by JAX's collectives and lax.ppermute only.
A program may use at most 128 MiB of HBM per device.

```python
import math
import jax
import jax.numpy as jnp
import numpy as np
from jax import lax

NODE_DEV = 8192
TILE = 128
NODES = 262144
ELEMS = 262144
HALO = 128
CAP = 512
FACE_DEV = 2048
FACES = 65536
GHOST = 256
NODE_TILES = 128
FACE_TILES = 20
PAIRS = 128
N_DOM = 8
N_SUB = 4
DEVICES = 32


def draw_connectivity(key, part):
    groups = ELEMS // NODE_DEV
    owner_dev = jnp.arange(ELEMS, dtype=jnp.int32) // NODE_DEV
    local = jnp.arange(ELEMS, dtype=jnp.int32) % NODE_DEV
    lower = jnp.where(owner_dev == 0, jnp.maximum(HALO - local, 0), 0)
    upper = jnp.where(owner_dev == groups - 1, jnp.minimum(2 * HALO - 2, NODE_DEV + HALO - 3 - local), 2 * HALO - 2)
    offset = jax.random.randint(key, (ELEMS,), lower, upper)
    base = local + offset
    corners = jnp.array([0, 1, 2, 3], dtype=jnp.int32)
    return (base[None, :] + corners[:, None]).astype(jnp.int32)


def draw_pair_count(key, part):
    groups = N_DOM * N_SUB
    halving = jax.random.randint(jax.random.fold_in(key, 11), (groups,), 0, 4)
    counts = PAIRS // 2 ** halving
    fullest = jax.random.randint(jax.random.fold_in(key, 12), (), 0, groups)
    return counts.at[fullest].set(PAIRS).astype(jnp.int32)


def with_ends(values, own_key, low, top_value):
    spot = [jax.random.randint(jax.random.fold_in(own_key, axis), (), 0, length) for axis, length in enumerate(values.shape)]
    main_axis = values.shape.index(max(values.shape))
    beside = spot[:main_axis] + [(spot[main_axis] + 1) % values.shape[main_axis]] + spot[main_axis + 1:]
    return values.at[tuple(spot)].set(low).at[tuple(beside)].set(top_value)


def shard_levels(own_key, dims, split, least, high):
    factor_of, own = 1.0, jax.random.fold_in(own_key, 6)
    for axis_at, blocks in split:
        heights = jnp.exp(jax.random.uniform(jax.random.fold_in(own, axis_at), (blocks,), jnp.float32, least / len(split), high / len(split)))
        factor_of = factor_of * jnp.repeat(heights, dims[axis_at] // blocks).reshape([-1 if axis == axis_at else 1 for axis in range(len(dims))])
    return factor_of


def shared_out(own_key, own, number, rows, amount, top, most, skew):
    sequence = jax.random.permutation(own_key, amount)
    heavy_load, ordinary = portions_of(amount, rows * top, most, skew, True), portions_of(amount, rows * top, most, skew, False)
    places = jnp.arange(amount)

    def named(lengths, turn):
        used = int((lengths > 0).sum())
        fixed = max(1, used // 4)
        shifted = fixed + (places - fixed + turn * (used - fixed)) % max(1, amount - fixed)
        return jnp.zeros((amount,), jnp.int32).at[sequence[jnp.where(places < fixed, places, shifted)]].set(jnp.asarray(lengths, jnp.int32))

    lengths = jnp.where(number % 4 == 0, named(heavy_load, number // 4), named(ordinary, number - number // 4 - 1))
    mixed = jax.random.permutation(jax.random.fold_in(own, 3), amount)
    donor, receiver = mixed[0:amount // 2 * 2:2], mixed[1:amount // 2 * 2:2]
    room = jnp.minimum(lengths[donor] - 1, most - lengths[receiver]) // 2
    room = jnp.where((donor == sequence[0]) | (receiver == sequence[0]) | (lengths[receiver] == 0), 0, jnp.maximum(room, 0))
    shifted = jax.random.randint(jax.random.fold_in(own, 4), (amount // 2,), 0, 1 << 20) % (room + 1)
    lengths = lengths.at[donor].add(-shifted).at[receiver].add(shifted)
    members = jnp.searchsorted(jnp.cumsum(lengths), jnp.arange(rows * top), side="right").astype(jnp.int32)
    listing = members.reshape(top, rows).T
    listing = listing[jax.random.permutation(jax.random.fold_in(own, 1), rows)]
    turn = jax.random.randint(jax.random.fold_in(own, 2), (rows, 1), 0, top)
    return jnp.take_along_axis(listing, (jnp.arange(top)[None, :] + turn) % top, axis=1)


def portions_of(count, total, most, skew, full):
    portions = [(1 << 20) // math.isqrt(grade ** skew) + 1 for grade in range(1, count + 1)]
    largest = most if full else min(most, max(-(-total // count), total * portions[0] // sum(portions)))
    least = 1 if total - largest >= count - 1 else 0
    given, spare = [largest] + [least] * (count - 1), total - largest - least * (count - 1)
    while spare > 0:
        movable = [i for i in range(1, count) if given[i] < largest] or [i for i in range(1, count) if given[i] < most]
        whole, budget = sum([portions[i] for i in movable]), spare
        for i in movable:
            addition = min(most - given[i], max(1, budget * portions[i] // whole), spare)
            given[i] = given[i] + addition
            spare = spare - addition
    return np.array(given)


def centred(rng, shape, spread, limit, pieces=(), kind=jnp.bfloat16):
    result = jax.random.normal(rng, shape, jnp.float32) * spread
    if len(pieces) > 0:
        result = shard_levels(rng, shape, pieces, -0.22, 0.18) * result
    return jnp.clip(result, min=-limit, max=limit).astype(kind)


def setup_inputs(seed: int = 0) -> dict:
    key_of = jax.random.split(jax.random.key(seed), 18)
    velocity = centred(key_of[0], (5, NODES), 1.0, 6.0, ((1, 32),), jnp.float32)
    position = jnp.clip(1.0 * jax.random.uniform(key_of[1], (3, NODES), jnp.float32) ** shard_levels(key_of[1], (3, NODES), ((1, 32),), -0.2, 0.2), 0.0, 1.0)
    inv_mass = jnp.clip(jnp.exp(math.log(0.3) - 1.7917595 * jax.random.uniform(key_of[2], (NODES,), jnp.float32) ** shard_levels(key_of[2], (NODES,), ((0, 32),), -0.2, 0.2)), 0.05, 0.3)
    connectivity = draw_connectivity(jax.random.fold_in(key_of[17], 71), 0)
    shape_grad = centred(key_of[4], (2, 4, ELEMS), 0.5, 3.0, ((2, 32),), jnp.float32)
    area = jnp.clip(jnp.exp(math.log(2.0) - 1.3862944 * jax.random.uniform(key_of[5], (ELEMS,), jnp.float32) ** shard_levels(key_of[5], (ELEMS,), ((0, 32),), -0.2, 0.2)), 0.5, 2.0)
    thickness = jnp.clip(0.5 + 1.0 * jax.random.uniform(key_of[6], (ELEMS,), jnp.float32) ** shard_levels(key_of[6], (ELEMS,), ((0, 32),), -0.2, 0.2), 0.5, 1.5)
    yield_stress = jnp.clip(jnp.exp(math.log(3.0) - 1.7917595 * jax.random.uniform(key_of[7], (ELEMS,), jnp.float32) ** shard_levels(key_of[7], (ELEMS,), ((0, 32),), -0.2, 0.2)), 0.5, 3.0)
    stress = centred(key_of[8], (5, 5, ELEMS), 1.0, 6.0, ((2, 32),), jnp.float32)
    contact_owner_keys = jax.random.split(jax.random.fold_in(key_of[9], 1), NODES // NODE_DEV)
    contact_owner_turns = jax.random.permutation(jax.random.fold_in(key_of[9], 3), NODES // NODE_DEV)
    contact_owner = jax.vmap(lambda own, number: shared_out(jax.random.fold_in(key_of[9], 2), own, number, NODE_DEV, DEVICES, 1, CAP, 2))(contact_owner_keys, contact_owner_turns).reshape((NODES, 1))
    face_center = jnp.clip(1.0 * jax.random.uniform(key_of[10], (3, FACES), jnp.float32) ** shard_levels(key_of[10], (3, FACES), ((1, 32),), -0.2, 0.2), 0.0, 1.0)
    face_angle = jnp.clip(jax.random.uniform(key_of[11], (2, FACES), jnp.float32, -3.140625, 3.140625), -3.140625, 3.140625)
    face_stiffness = jnp.clip(jnp.exp(math.log(10.0) - 2.3025851 * jax.random.uniform(key_of[12], (FACES,), jnp.float32) ** shard_levels(key_of[12], (FACES,), ((0, 32),), -0.2, 0.2)), 1.0, 10.0)
    ghost_list = with_ends(jax.random.randint(key_of[13], (2 * GHOST * DEVICES,), 0, FACE_DEV), jax.random.fold_in(key_of[13], 1), 0, FACE_DEV - 1).astype(jnp.int32)
    pair_node = with_ends(jax.random.randint(key_of[14], (PAIRS * DEVICES,), 0, NODE_TILES), jax.random.fold_in(key_of[14], 1), 0, NODE_TILES - 1).astype(jnp.int32)
    pair_face = with_ends(jax.random.randint(key_of[15], (PAIRS * DEVICES,), 0, FACE_TILES), jax.random.fold_in(key_of[15], 1), 0, FACE_TILES - 1).astype(jnp.int32)
    pair_count = draw_pair_count(jax.random.fold_in(key_of[17], 71), 0)
    return dict(velocity=velocity, position=position, inv_mass=inv_mass, connectivity=connectivity, shape_grad=shape_grad, area=area, thickness=thickness, yield_stress=yield_stress, stress=stress, contact_owner=contact_owner, face_center=face_center, face_angle=face_angle, face_stiffness=face_stiffness, ghost_list=ghost_list, pair_node=pair_node, pair_face=pair_face, pair_count=pair_count)


LOBATTO_POINTS = (-1.0, -0.6546536707079771, 0.0, 0.6546536707079771, 1.0)
LOBATTO_WEIGHTS = (0.1, 49.0 / 90.0, 32.0 / 45.0, 49.0 / 90.0, 0.1)
PLANE_MODULUS = 1.0 / 0.91
POISSON = 0.3
SHEAR_MODULUS = 5.0 / 6.0 / 2.6
DAMPING = 0.3
REACH_SQ = 0.5

def element_forces(corner, grads, area, thickness, yield_stress, old_stress):
    vel_x, vel_y, vel_z, rot_x, rot_y = (corner[0], corner[1], corner[2], corner[3], corner[4])
    grad_x, grad_y = (grads[0], grads[1])
    memb_xx = lax.optimization_barrier(jnp.sum(grad_x * vel_x, axis=0))
    bend_xx = lax.optimization_barrier(jnp.sum(grad_x * rot_y, axis=0))
    memb_yy = lax.optimization_barrier(jnp.sum(grad_y * vel_y, axis=0))
    bend_yy = -lax.optimization_barrier(jnp.sum(grad_y * rot_x, axis=0))
    memb_xy = lax.optimization_barrier(jnp.sum(grad_y * vel_x + grad_x * vel_y, axis=0))
    bend_xy = lax.optimization_barrier(jnp.sum(grad_y * rot_y - grad_x * rot_x, axis=0))
    shear_xz = lax.optimization_barrier(jnp.sum(grad_x * vel_z, axis=0)) + 0.25 * lax.optimization_barrier(jnp.sum(rot_y, axis=0))
    shear_yz = lax.optimization_barrier(jnp.sum(grad_y * vel_z, axis=0)) - 0.25 * lax.optimization_barrier(jnp.sum(rot_x, axis=0))
    layers = []
    membrane = []
    moments = []
    for layer in range(5):
        height = 0.5 * thickness * LOBATTO_POINTS[layer]
        strain_xx = memb_xx + height * bend_xx
        strain_yy = memb_yy + height * bend_yy
        strain_xy = memb_xy + height * bend_xy
        trial_xx = old_stress[layer, 0] + PLANE_MODULUS * (strain_xx + POISSON * strain_yy)
        trial_yy = old_stress[layer, 1] + PLANE_MODULUS * (strain_yy + POISSON * strain_xx)
        trial_xy = old_stress[layer, 2] + PLANE_MODULUS * 0.5 * (1.0 - POISSON) * strain_xy
        trial_xz = old_stress[layer, 3] + SHEAR_MODULUS * shear_xz
        trial_yz = old_stress[layer, 4] + SHEAR_MODULUS * shear_yz
        mises = jnp.sqrt(0.25 * (trial_xx + trial_yy) ** 2 + 0.75 * (trial_xx - trial_yy) ** 2 + 3.0 * (trial_xy ** 2 + trial_xz ** 2 + trial_yz ** 2))
        factor = yield_stress / jnp.maximum(mises, yield_stress)
        updated = jnp.stack([trial_xx, trial_yy, trial_xy, trial_xz, trial_yz]) * factor
        layers.append(updated)
        weight = LOBATTO_WEIGHTS[layer] * 0.5 * thickness * area
        membrane.append(weight * updated)
        moments.append(weight * height * updated[0:3])
    new_stress = jnp.stack(layers)
    force_sum = sum(membrane)
    moment_sum = sum(moments)
    force_x = grad_x * force_sum[0] + grad_y * force_sum[2]
    force_y = grad_y * force_sum[1] + grad_x * force_sum[2]
    force_z = grad_x * force_sum[3] + grad_y * force_sum[4]
    moment_x = -(grad_y * moment_sum[1] + grad_x * moment_sum[2]) - 0.25 * force_sum[4]
    moment_y = grad_x * moment_sum[0] + grad_y * moment_sum[2] + 0.25 * force_sum[3]
    return (jnp.stack([force_x, force_y, force_z, moment_x, moment_y]), new_stress)

def slot_ranks(target, number):
    ordering = jnp.argsort(target, stable=True).astype(jnp.int32)
    ordered = target[ordering]
    totals = jnp.bincount(target, length=number).astype(jnp.int32)
    starts = jnp.cumsum(totals).astype(jnp.int32) - totals
    within = jnp.arange(target.shape[0], dtype=jnp.int32) - starts[ordered]
    return jnp.zeros(target.shape[0], jnp.int32).at[ordering].set(within)

def face_normals(face_angle):
    azimuth, elevation = (face_angle[0], face_angle[1])
    return jnp.stack([jnp.cos(azimuth) * jnp.cos(elevation), jnp.sin(azimuth) * jnp.cos(elevation), jnp.sin(elevation)])

def pair_forces(node_block, face_block, live):
    offset = node_block[0:3, :, :, None] - face_block[0:3, :, None, :]
    normal = face_block[3:6, :, None, :]
    depth = jnp.maximum(-lax.optimization_barrier(jnp.sum(normal * offset, axis=0)), 0.0)
    reach = jnp.exp(-lax.optimization_barrier(jnp.sum(offset * offset, axis=0)) / REACH_SQ)
    along = lax.optimization_barrier(jnp.sum(normal * node_block[3:6, :, :, None], axis=0))
    magnitude = face_block[6][:, None, :] * reach * depth * (1.0 - DAMPING * along)
    magnitude = magnitude * node_block[6][:, :, None] * live[:, None, None]
    return jnp.einsum('bij,cbj->cbi', magnitude, face_block[3:6], precision=lax.Precision.HIGHEST)

def reference(velocity, position, inv_mass, connectivity, shape_grad, area, thickness, yield_stress, stress, contact_owner, face_center, face_angle, face_stiffness, ghost_list, pair_node, pair_face, pair_count):
    devices = N_DOM * N_SUB
    capacity = 2 * NODE_DEV // devices
    ftype = velocity.dtype
    owner_dev = (jnp.arange(ELEMS, dtype=jnp.int32) // NODE_DEV).astype(jnp.int32)
    gnode = (owner_dev[None, :] * NODE_DEV + connectivity - HALO).astype(jnp.int32)

    def per_device(inputs):
        nodes_of, grads, area_of, thick_of, yield_of, stress_of = inputs
        return element_forces(velocity[:, nodes_of], grads, area_of, thick_of, yield_of, stress_of)
    forces, new_stress = lax.map(per_device, (gnode.reshape(4, devices, NODE_DEV).transpose(1, 0, 2), shape_grad.reshape(2, 4, devices, NODE_DEV).transpose(2, 0, 1, 3), area.reshape(devices, NODE_DEV), thickness.reshape(devices, NODE_DEV), yield_stress.reshape(devices, NODE_DEV), stress.reshape(5, 5, devices, NODE_DEV).transpose(2, 0, 1, 3)))
    forces = forces.transpose(1, 2, 0, 3).reshape(5, 4, ELEMS)
    new_stress = new_stress.transpose(1, 2, 0, 3).reshape(5, 5, ELEMS)
    internal = jnp.zeros_like(velocity).at[:, gnode].add(forces)
    owner = contact_owner[:, 0].reshape(devices, NODE_DEV)
    ranks = lax.map(lambda target: slot_ranks(target, devices), owner)
    source = jnp.arange(devices, dtype=jnp.int32)[:, None]
    gslot = (owner * (devices * capacity) + source * capacity + ranks).reshape(-1)
    payload = jnp.concatenate([position, velocity[0:3], jnp.ones((1, NODES), ftype)], axis=0)
    received = jnp.zeros((7, devices * devices * capacity), ftype).at[:, gslot].set(payload)
    received = received.reshape(7, devices, devices * capacity).transpose(1, 0, 2)
    face_data = jnp.concatenate([face_center, face_normals(face_angle), face_stiffness[None, :]], axis=0)
    by_dev = face_data.reshape(7, devices, FACE_DEV)
    lists = ghost_list.reshape(devices, 2 * GHOST)
    lent = jnp.take_along_axis(by_dev, lists[None, :, :], axis=2)
    blank = jnp.zeros((7, 1, GHOST), ftype)
    from_prev = jnp.concatenate([blank, lent[:, :-1, GHOST:]], axis=1)
    from_next = jnp.concatenate([lent[:, 1:, :GHOST], blank], axis=1)
    faces_all = jnp.concatenate([from_prev, by_dev, from_next], axis=2).transpose(1, 0, 2)
    block = 64 if PAIRS % 64 == 0 else 8
    node_pairs = pair_node.reshape(devices, PAIRS)
    face_pairs = pair_face.reshape(devices, PAIRS)

    def contact_device(inputs):
        nodes_of, faces_of, pnodes, pfaces, live_count = inputs
        node_tiles = nodes_of.reshape(7, NODE_TILES, TILE)
        face_tiles = faces_of.reshape(7, FACE_TILES, TILE)

        def per_block(index):
            start = index * block
            pn = lax.dynamic_slice_in_dim(pnodes, start, block)
            pf = lax.dynamic_slice_in_dim(pfaces, start, block)
            live = (start + jnp.arange(block, dtype=jnp.int32) < live_count).astype(ftype)
            return pair_forces(jnp.take(node_tiles, pn, axis=1), jnp.take(face_tiles, pf, axis=1), live)
        parts = lax.map(per_block, jnp.arange(PAIRS // block, dtype=jnp.int32))
        parts = parts.transpose(0, 2, 1, 3).reshape(PAIRS, 3, TILE)
        summed = jax.ops.segment_sum(parts, pnodes, num_segments=NODE_TILES)
        return summed.transpose(1, 0, 2).reshape(3, NODE_TILES * TILE)
    contact_all = lax.map(contact_device, (received, faces_all, node_pairs, face_pairs, pair_count))
    contact = contact_all.transpose(1, 0, 2).reshape(3, -1)[:, gslot]
    total = (-internal).at[0:3].add(contact)
    new_velocity = velocity + inv_mass[None, :] * total
    return (new_velocity, new_stress)
```

```python
import functools

import jax
import jax.numpy as jnp
from jax import lax
from jax.experimental import pallas as pl
from jax.experimental.pallas import tpu as pltpu
from jax.sharding import PartitionSpec as P

LANES = 128
HALO = 128
GHOST = 256
LOW = 64

LOBATTO_POINTS = (-1.0, -0.6546536707079771, 0.0, 0.6546536707079771, 1.0)
LOBATTO_WEIGHTS = (0.1, 49.0 / 90.0, 32.0 / 45.0, 49.0 / 90.0, 0.1)
PLANE_MODULUS = 1.0 / 0.91
POISSON = 0.3
SHEAR_MODULUS = 5.0 / 6.0 / 2.6
DAMPING = 0.3
REACH_SQ = 0.5
LOG2E = 1.4426950408889634

F32 = jnp.float32
BF16 = jnp.bfloat16
NT = (((1,), (1,)), ((), ()))
NN = (((1,), (0,)), ((), ()))


def iota(shape, dim):
    return lax.broadcasted_iota(jnp.int32, shape, dim)


def split2(x):
    high = x.astype(BF16).astype(F32)
    return high, x - high


def tiled_rows(row, count):
    packed = jnp.broadcast_to(row, (16, row.shape[1])).astype(BF16)
    return packed if count == 16 else jnp.concatenate([packed] * (count // 16), axis=0)


def arrange_kernel(owner, position, velocity, out, slot_out, lhs, rhs, acc, *, devices, capacity):
    rows = owner.shape[0]
    tiles = capacity // LANES
    upper = jnp.where(iota((LANES, 2 * LANES), 1) > iota((LANES, 2 * LANES), 0), 1.0, 0.0).astype(BF16)
    device_ids = iota((devices, LANES), 0)
    low_ids = iota((LOW, LANES), 0).astype(F32).astype(BF16)
    group_ids = iota((2 * LANES, LANES), 0).astype(F32).astype(BF16)
    acc[...] = jnp.zeros_like(acc)
    one, zero = jnp.ones((), BF16), jnp.zeros((), BF16)

    def step(k, base):
        owners = owner[pl.ds(pl.multiple_of(k * 8, 8), 8), :]
        masks = [jnp.broadcast_to(owners[s : s + 1], (devices, LANES)) == device_ids for s in range(8)]
        hot = jnp.concatenate([jnp.where(m, 1.0, 0.0).astype(BF16) for m in masks], axis=0)
        counted = lax.dot_general(hot, upper, NN, preferred_element_type=F32)
        ranks = []
        for s in range(8):
            part = counted[s * devices : (s + 1) * devices]
            ranks.append(jnp.sum(jnp.where(masks[s], part[:, :LANES] + base, 0.0), axis=0, keepdims=True))
            base = base + part[:, LANES:]
        rank = jnp.concatenate(ranks, axis=0).astype(jnp.int32)
        slot = owners * capacity + rank
        slot_out[pl.ds(pl.multiple_of(k * 8, 8), 8), :] = slot
        low = (slot & (LOW - 1)).astype(F32)
        group = (((slot >> 6) & 1) * LANES + (slot >> 7)).astype(F32)
        for s in range(8):
            lanes = pl.ds(pl.multiple_of(k * 8 * LANES + s * LANES, LANES), LANES)
            here = pl.ds(s * LANES, LANES)
            hot_low = jnp.where(tiled_rows(low[s : s + 1], LOW) == low_ids, one, zero)
            rhs[:, here] = jnp.where(tiled_rows(group[s : s + 1], 2 * LANES) == group_ids, one, zero)
            place = position[:, lanes]
            place = place + jnp.where(iota(place.shape, 0) == 0, 1.0, 0.0)
            for base_row, data in ((0, place), (3, velocity[0:3, lanes])):
                parts = split2(data)
                for c in range(3):
                    for half in range(2):
                        row = (base_row + c) * 2 + half
                        lhs[row * LOW : (row + 1) * LOW, here] = hot_low * tiled_rows(parts[half][c : c + 1], LOW)
        acc[...] += lax.dot_general(lhs[...], rhs[...], NT, preferred_element_type=F32)
        return base

    lax.fori_loop(0, rows // 8, step, jnp.zeros((devices, LANES), F32))
    for c in range(6):
        both = acc[2 * c * LOW : (2 * c + 1) * LOW, :] + acc[(2 * c + 1) * LOW : (2 * c + 2) * LOW, :]
        square = jnp.concatenate([both[:, :LANES], both[:, LANES:]], axis=0).T
        out[:, c * tiles : (c + 1) * tiles, :] = square.reshape(devices, tiles, LANES)


def face_kernel(center, angle, stiffness, ghost, velocity, slot, own, up, down):
    del slot
    count = stiffness.shape[0]
    faces = count * LANES
    azimuth = angle[0, :].reshape(count, LANES)
    elevation = angle[1, :].reshape(count, LANES)
    flat = jnp.cos(elevation)
    data = [center[c, :].reshape(count, LANES) for c in range(3)]
    data += [jnp.cos(azimuth) * flat, jnp.sin(azimuth) * flat, jnp.sin(elevation), stiffness[...]]
    wanted = ghost[...]
    wanted = jnp.concatenate([wanted, wanted], axis=0)
    row_of, lane_of = wanted >> 7, wanted & (LANES - 1)
    nodes = velocity.shape[1]
    up[...] = jnp.zeros_like(up)
    down[...] = jnp.zeros_like(down)
    up[0:5, :] = velocity[:, nodes - HALO :]
    down[0:5, :] = velocity[:, :HALO]
    for c in range(8):
        if c == 7:
            own[pl.ds(c, count, stride=8), :] = jnp.zeros((count, LANES), F32)
            continue
        own[pl.ds(c, count, stride=8), :] = data[c]
        found = jnp.zeros((8, LANES), F32)
        for r in range(count):
            source = jnp.broadcast_to(data[c][r : r + 1], (8, LANES))
            found = jnp.where(row_of == r, jnp.take_along_axis(source, lane_of, axis=1), found)
        for t in range(2):
            down[8 + 8 * t + c : 9 + 8 * t + c, :] = found[t : t + 1]
            up[8 + 8 * t + c : 9 + 8 * t + c, :] = found[2 + t : 3 + t]


def element_kernel(
    velocity, before, after, connectivity, grads, area, thickness, yields, stress,
    new_stress, own, rim_down, rim_up, ext, spread, where_row, where_lane, acc,
):
    nodes = velocity.shape[1]
    rows = nodes // LANES
    pitch = ext.shape[0] // 5
    chunk = 8 * LANES
    for c in range(5):
        ext[c * pitch : c * pitch + 1, :] = before[c : c + 1, :]
        for k in range(rows // 8):
            ext[c * pitch + 1 + 8 * k : c * pitch + 9 + 8 * k, :] = velocity[c, pl.ds(k * chunk, chunk)].reshape(8, LANES)
        ext[c * pitch + rows + 1 : c * pitch + rows + 2, :] = after[c : c + 1, :]
    for a in range(4):
        spread[(a * 8 + 5) * rows : (a * 8 + 8) * rows, :] = jnp.zeros((3 * rows, LANES), F32)
    acc[...] = jnp.zeros_like(acc)

    def elements(k, carry):
        here = pl.ds(pl.multiple_of(k * chunk, chunk), chunk)
        first = pl.multiple_of(k * 8, 8)
        packed = pl.ds(first, 8)
        sources = [[ext[pl.ds(c * pitch + k * 8 + j, 8), :] for j in range(3)] for c in range(5)]
        row_ids = iota((8, LANES), 0) + k * 8
        corner = []
        for a in range(4):
            index = connectivity[a, here].reshape(8, LANES)
            lane = index & (LANES - 1)
            rel = (index >> 7) - row_ids
            where_lane[pl.ds(a * rows + first, 8), :] = lane.astype(F32)
            where_row[pl.ds(a * rows + first, 8), :] = rel.astype(F32)
            second, third = rel == 1, rel == 2
            values = []
            for c in range(5):
                g = [jnp.take_along_axis(sources[c][j], lane, axis=1) for j in range(3)]
                values.append(jnp.where(third, g[2], jnp.where(second, g[1], g[0])))
            corner.append(values)
        gx = [grads[0, a, here].reshape(8, LANES) for a in range(4)]
        gy = [grads[1, a, here].reshape(8, LANES) for a in range(4)]

        def total(f):
            t = [f(a) for a in range(4)]
            return (t[0] + t[1]) + (t[2] + t[3])

        memb_xx = total(lambda a: gx[a] * corner[a][0])
        bend_xx = total(lambda a: gx[a] * corner[a][4])
        memb_yy = total(lambda a: gy[a] * corner[a][1])
        bend_yy = -total(lambda a: gy[a] * corner[a][3])
        memb_xy = total(lambda a: gy[a] * corner[a][0] + gx[a] * corner[a][1])
        bend_xy = total(lambda a: gy[a] * corner[a][4] - gx[a] * corner[a][3])
        shear_xz = total(lambda a: gx[a] * corner[a][2]) + 0.25 * total(lambda a: corner[a][4])
        shear_yz = total(lambda a: gy[a] * corner[a][2]) - 0.25 * total(lambda a: corner[a][3])
        thick = thickness[packed, :]
        limit = yields[packed, :]
        half_area = 0.5 * thick * area[packed, :]
        force = [None] * 5
        moment = [None] * 3
        for layer in range(5):
            height = (0.5 * LOBATTO_POINTS[layer]) * thick
            xx = memb_xx + height * bend_xx
            yy = memb_yy + height * bend_yy
            xy = memb_xy + height * bend_xy
            old = [stress[layer, c, here].reshape(8, LANES) for c in range(5)]
            t = [
                old[0] + PLANE_MODULUS * (xx + POISSON * yy),
                old[1] + PLANE_MODULUS * (yy + POISSON * xx),
                old[2] + (PLANE_MODULUS * 0.5 * (1.0 - POISSON)) * xy,
                old[3] + SHEAR_MODULUS * shear_xz,
                old[4] + SHEAR_MODULUS * shear_yz,
            ]
            plus, minus = t[0] + t[1], t[0] - t[1]
            mises = jnp.sqrt(
                0.25 * (plus * plus) + 0.75 * (minus * minus) + 3.0 * (t[2] * t[2] + t[3] * t[3] + t[4] * t[4])
            )
            factor = limit / jnp.maximum(mises, limit)
            weight = LOBATTO_WEIGHTS[layer] * half_area
            lever = weight * height
            for c in range(5):
                value = t[c] * factor
                new_stress[layer, c, here] = value.reshape(chunk)
                term = weight * value
                force[c] = term if layer == 0 else force[c] + term
                if c < 3 and layer != 2:
                    term = lever * value
                    moment[c] = term if layer == 0 else moment[c] + term
        for a in range(4):
            out = (
                gx[a] * force[0] + gy[a] * force[2],
                gy[a] * force[1] + gx[a] * force[2],
                gx[a] * force[3] + gy[a] * force[4],
                -(gy[a] * moment[1] + gx[a] * moment[2]) - 0.25 * force[4],
                gx[a] * moment[0] + gy[a] * moment[2] + 0.25 * force[3],
            )
            for c in range(5):
                spread[pl.ds((a * 8 + c) * rows + first, 8), :] = out[c]
        return carry

    lax.fori_loop(0, rows // 8, elements, 0)
    lane_ids = iota((LANES, LANES), 0).astype(F32).astype(BF16)
    one, zero = jnp.ones((), BF16), jnp.zeros((), BF16)

    def scatter_row(b):
        left, right = [], []
        for a in range(4):
            data = spread[pl.ds(a * 8 * rows + b, 8, stride=rows), :]
            high, low = split2(data)
            both = jnp.concatenate([high, low], axis=0).astype(BF16)
            rel = tiled_rows(where_row[pl.ds(a * rows + b, 1), :], 16)
            left.append(jnp.concatenate([jnp.where(rel == jnp.asarray(j, BF16), both, zero) for j in range(3)], axis=0))
            lane = tiled_rows(where_lane[pl.ds(a * rows + b, 1), :], LANES)
            right.append(jnp.where(lane == lane_ids, one, zero))
        out = lax.dot_general(
            jnp.concatenate(left, axis=1), jnp.concatenate(right, axis=1), NT, preferred_element_type=F32
        )
        return [out[16 * j : 16 * j + 8] + out[16 * j + 8 : 16 * j + 16] for j in range(3)]

    def scatter(step, carry):
        b = step * 4
        parts = [scatter_row(b + i) for i in range(4)]
        for i in range(4):
            for j in range(3):
                at = pl.ds(pl.multiple_of((b + i + j) * 8, 8), 8)
                acc[at, :] += parts[i][j]
        return carry

    lax.fori_loop(0, rows // 4, scatter, 0)
    rim_down[...] = acc[0:8, :]
    own[...] = acc[8 : 8 + 8 * rows, :]
    rim_up[...] = acc[8 + 8 * rows : 16 + 8 * rows, :]


def contact_kernel(pair_node, pair_face, pair_count, nodes, own, before, after, out, raw, face, normal, acc, *, devices, tiles):
    own_rows = own.shape[0]
    face_tiles = (own_rows + 32) // 8
    raw[0:16, :] = before[8:24, :]
    raw[16 : 16 + own_rows, :] = own[...]
    raw[16 + own_rows :, :] = after[8:24, :]
    sub = iota((8, LANES), 0)

    def prepare(f, carry):
        at = pl.multiple_of(f * 8, 8)
        data = raw[pl.ds(at, 8), :]
        centre = data - 0.5
        mean = [jnp.broadcast_to(data[3 + c : 4 + c], (8, LANES)) for c in range(3)]
        place = [jnp.broadcast_to(centre[c : c + 1], (8, LANES)) for c in range(3)]
        stiff = jnp.broadcast_to(data[6:7], (8, LANES))
        m_low = jnp.where(sub == 0, mean[0], jnp.where(sub == 1, mean[1], jnp.where(sub == 2, mean[2], 0.0)))
        coef_e = jnp.where(sub < 3, (2.0 / REACH_SQ * LOG2E) * centre, jnp.where(sub == 6, 1.0, 0.0))
        coef_d = -m_low
        coef_a = jnp.where((sub >= 3) & (sub < 6), (-DAMPING) * stiff * data, jnp.where(sub == 7, stiff, 0.0))
        square = place[0] * place[0] + place[1] * place[1] + place[2] * place[2]
        along = mean[0] * place[0] + mean[1] * place[1] + mean[2] * place[2]
        pieces = []
        for coef, const in ((coef_e, (-LOG2E / REACH_SQ) * square), (coef_d, along), (coef_a, None)):
            high, low = split2(coef)
            if const is None:
                last = jnp.zeros((8, LANES), F32)
            else:
                c_high, c_low = split2(const)
                last = jnp.where(sub == 0, c_high, jnp.where(sub == 1, c_low, 0.0))
            pieces.append(jnp.concatenate([high, high, low, last], axis=0).astype(BF16))
        face[pl.ds(pl.multiple_of(f * 32, 32), 32), :] = jnp.concatenate(pieces, axis=1)
        high, low = split2(m_low)
        top = jnp.concatenate([high, low], axis=0).astype(BF16)
        bottom = jnp.concatenate([high, jnp.zeros_like(high)], axis=0).astype(BF16)
        normal[pl.ds(pl.multiple_of(f * 16, 16), 16), :] = jnp.concatenate([top, bottom], axis=1)
        return carry

    lax.fori_loop(0, face_tiles, prepare, 0)
    acc[...] = jnp.zeros_like(acc)
    shift = jnp.where(iota((6, LANES), 0) == 0, 1.5, jnp.where(iota((6, LANES), 0) < 3, 0.5, 0.0))
    ones = jnp.ones((8, LANES), F32)

    def pair_force(node, which):
        source = node // tiles
        data = nodes[pl.ds(source * (6 * tiles) + (node - source * tiles), 6, stride=tiles), :]
        live = jnp.where(data[0:1] > 0.5, 1.0, 0.0)
        data = data - shift
        square = data * data
        square = square[0:1] + square[1:2] + square[2:3]
        full = jnp.concatenate([data, (-LOG2E / REACH_SQ) * square, live], axis=0)
        high, low = split2(full)
        matrix = jnp.concatenate([high, low, high, ones], axis=0).T.astype(BF16)
        at = pl.ds(pl.multiple_of(which * 32, 32), 32)
        terms = lax.dot_general(matrix, face[at, :], NN, preferred_element_type=F32)
        power, depth, scale = terms[:, :LANES], terms[:, LANES : 2 * LANES], terms[:, 2 * LANES :]
        magnitude = jnp.exp2(power) * jnp.maximum(depth, 0.0) * scale
        high = magnitude.astype(BF16)
        low = (magnitude - high.astype(F32)).astype(BF16)
        both = jnp.concatenate([high, low], axis=1)
        at = pl.ds(pl.multiple_of(which * 16, 16), 16)
        result = lax.dot_general(normal[at, :], both, NT, preferred_element_type=F32)
        return result[0:8] + result[8:16]

    count = pair_count[0]
    group = 4

    def step(i, carry):
        ids = [i * group + n for n in range(group)]
        at = [pair_node[q] for q in ids]
        found = [pair_force(at[n], pair_face[ids[n]]) for n in range(group)]
        for n in range(group):
            keep = jnp.where(ids[n] < count, 1.0, 0.0)
            rows = pl.ds(pl.multiple_of(at[n] * 8, 8), 8)
            acc[rows, :] += found[n] * keep
        return carry

    lax.fori_loop(0, (count + group - 1) // group, step, 0)
    total = devices * tiles
    for c in range(3):
        out[:, c * tiles : (c + 1) * tiles, :] = acc[pl.ds(c, total, stride=8), :].reshape(devices, tiles, LANES)


def final_kernel(back, slot, own, below, above, velocity, inv_mass, out, table, *, tiles):
    devices = back.shape[0]
    rows = slot.shape[0]
    for c in range(3):
        square = back[:, c * tiles : (c + 1) * tiles, :].reshape(devices * tiles, LANES).T
        wide = jnp.concatenate([square[:LOW], square[LOW:]], axis=1)
        high, low = split2(wide)
        table[2 * c * LOW : (2 * c + 1) * LOW, :] = high.astype(BF16)
        table[(2 * c + 1) * LOW : (2 * c + 2) * LOW, :] = low.astype(BF16)
    group_ids = iota((2 * LANES, LANES), 0).astype(F32).astype(BF16)
    low_ids = iota((LOW, LANES), 0)
    one, zero = jnp.ones((), BF16), jnp.zeros((), BF16)
    sub = iota((8, LANES), 0)

    def step(k, carry):
        slots = slot[pl.ds(pl.multiple_of(k * 8, 8), 8), :]
        low = slots & (LOW - 1)
        group = (((slots >> 6) & 1) * LANES + (slots >> 7)).astype(F32)
        for s in range(0, 8, 2):
            hot = [jnp.where(tiled_rows(group[i : i + 1], 2 * LANES) == group_ids, one, zero) for i in (s, s + 1)]
            picked = lax.dot_general(table[...], jnp.concatenate(hot, axis=1), NN, preferred_element_type=F32)
            for i in range(2):
                r = k * 8 + s + i
                mask = jnp.broadcast_to(low[s + i : s + i + 1], (LOW, LANES)) == low_ids
                contact = jnp.zeros((8, LANES), F32)
                for c in range(3):
                    part = picked[2 * c * LOW : (2 * c + 2) * LOW, i * LANES : (i + 1) * LANES]
                    value = jnp.sum(jnp.where(mask, part[:LOW] + part[LOW:], 0.0), axis=0, keepdims=True)
                    contact = jnp.where(sub == c, value, contact)
                lanes = pl.ds(pl.multiple_of(r * LANES, LANES), LANES)
                total = contact - own[pl.ds(pl.multiple_of(r * 8, 8), 8), :]
                out[:, lanes] = velocity[:, lanes] + inv_mass[pl.ds(r, 1), :] * total[0:5]
        return carry

    lax.fori_loop(0, rows // 8, step, 0)
    last = (rows - 1) * LANES
    out[:, 0:LANES] = out[:, 0:LANES] - inv_mass[0:1, :] * below[0:5, :]
    out[:, last:] = out[:, last:] - inv_mass[rows - 1 : rows, :] * above[0:5, :]


def call(kernel, outs, ins, scratch, cost, smem=0):
    vmem = pl.BlockSpec(memory_space=pltpu.VMEM)
    scalar = pl.BlockSpec(memory_space=pltpu.SMEM)
    return pl.pallas_call(
        kernel,
        out_shape=outs,
        in_specs=[scalar] * smem + [vmem] * (len(ins) - smem),
        out_specs=jax.tree.map(lambda _: vmem, outs),
        scratch_shapes=scratch,
        cost_estimate=pl.CostEstimate(flops=cost, bytes_accessed=cost // 100, transcendentals=0),
    )(*ins)


def body(
    velocity, position, inv_mass, connectivity, shape_grad, area, thickness, yield_stress, stress,
    contact_owner, face_center, face_angle, face_stiffness, ghost_list, pair_node, pair_face, pair_count,
):
    axes = ("dom", "sub")
    devices = lax.axis_size("dom") * lax.axis_size("sub")
    nodes = velocity.shape[1]
    faces = face_center.shape[1]
    rows = nodes // LANES
    capacity = 2 * nodes // devices
    tiles = capacity // LANES
    shape = lambda *s: jax.ShapeDtypeStruct(s, F32)
    view = lambda x: x.reshape(-1, LANES)

    outgoing, slot = call(
        functools.partial(arrange_kernel, devices=devices, capacity=capacity),
        (shape(devices, 6 * tiles, LANES), jax.ShapeDtypeStruct((rows, LANES), jnp.int32)),
        (view(contact_owner), position, velocity),
        [
            pltpu.VMEM((12 * LOW, 8 * LANES), BF16),
            pltpu.VMEM((2 * LANES, 8 * LANES), BF16),
            pltpu.VMEM((12 * LOW, 2 * LANES), F32),
        ],
        10**9,
    )
    incoming = lax.all_to_all(outgoing, axes, split_axis=0, concat_axis=0, tiled=True)
    own_faces, send_up, send_down = call(
        face_kernel,
        (shape(faces // LANES * 8, LANES), shape(24, LANES), shape(24, LANES)),
        (face_center, face_angle, view(face_stiffness), view(ghost_list), velocity, slot),
        [],
        10**8,
    )
    up = [(i, i + 1) for i in range(devices - 1)]
    down = [(j, i) for i, j in up]
    before = lax.ppermute(send_up, axes, up)
    after = lax.ppermute(send_down, axes, down)
    pitch = rows + 8
    new_stress, own, rim_down, rim_up = call(
        element_kernel,
        (shape(*stress.shape), shape(8 * rows, LANES), shape(8, LANES), shape(8, LANES)),
        (velocity, before, after, connectivity, shape_grad, view(area), view(thickness), view(yield_stress), stress),
        [
            pltpu.VMEM((5 * pitch, LANES), F32),
            pltpu.VMEM((4 * 8 * rows, LANES), F32),
            pltpu.VMEM((4 * rows, LANES), F32),
            pltpu.VMEM((4 * rows, LANES), F32),
            pltpu.VMEM((8 * (rows + 2), LANES), F32),
        ],
        2 * 10**9,
    )
    face_rows = own_faces.shape[0] + 32
    returned = call(
        functools.partial(contact_kernel, devices=devices, tiles=tiles),
        shape(devices, 3 * tiles, LANES),
        (pair_node, pair_face, pair_count, view(incoming), own_faces, before, after),
        [
            pltpu.VMEM((face_rows, LANES), F32),
            pltpu.VMEM((face_rows * 4, 3 * LANES), BF16),
            pltpu.VMEM((face_rows * 2, 2 * LANES), BF16),
            pltpu.VMEM((devices * tiles * 8, LANES), F32),
        ],
        10**9,
        smem=3,
    )
    back = lax.all_to_all(returned, axes, split_axis=0, concat_axis=0, tiled=True)
    above = lax.ppermute(rim_down, axes, down)
    below = lax.ppermute(rim_up, axes, up)
    new_velocity = call(
        functools.partial(final_kernel, tiles=tiles),
        shape(*velocity.shape),
        (back, slot, own, below, above, velocity, view(inv_mass)),
        [pltpu.VMEM((6 * LOW, 2 * LANES), BF16)],
        10**9,
    )
    return (new_velocity, new_stress)


def solution(mesh):
    split = ("dom", "sub")
    in_specs = (
        P(None, split), P(None, split), P(split), P(None, split), P(None, None, split),
        P(split), P(split), P(split), P(None, None, split), P(split, None),
        P(None, split), P(None, split), P(split), P(split), P(split), P(split), P(split),
    )
    out_specs = (P(None, split), P(None, None, split))
    return jax.shard_map(body, mesh=mesh, in_specs=in_specs, out_specs=out_specs, check_vma=False)
```

```python
import functools

import jax
import jax.numpy as jnp
from jax import lax
from jax.experimental import pallas as pl
from jax.experimental.pallas import tpu as pltpu
from jax.sharding import PartitionSpec as P

LANES = 128
HALO = 128
GHOST = 256
LOW = 64

LOBATTO_POINTS = (-1.0, -0.6546536707079771, 0.0, 0.6546536707079771, 1.0)
LOBATTO_WEIGHTS = (0.1, 49.0 / 90.0, 32.0 / 45.0, 49.0 / 90.0, 0.1)
PLANE_MODULUS = 1.0 / 0.91
POISSON = 0.3
SHEAR_MODULUS = 5.0 / 6.0 / 2.6
DAMPING = 0.3
REACH_SQ = 0.5
LOG2E = 1.4426950408889634

F32 = jnp.float32
BF16 = jnp.bfloat16
NT = (((1,), (1,)), ((), ()))
NN = (((1,), (0,)), ((), ()))


def iota(shape, dim):
    return lax.broadcasted_iota(jnp.int32, shape, dim)


def split2(x):
    high = x.astype(BF16).astype(F32)
    return high, x - high


def tiled_rows(row, count):
    packed = jnp.broadcast_to(row, (16, row.shape[1])).astype(BF16)
    return packed if count == 16 else jnp.concatenate([packed] * (count // 16), axis=0)


def arrange_kernel(owner, position, velocity, out, slot_out, lhs, rhs, acc, *, devices, capacity):
    rows = owner.shape[0]
    tiles = capacity // LANES
    upper = jnp.where(iota((LANES, 2 * LANES), 1) > iota((LANES, 2 * LANES), 0), 1.0, 0.0).astype(BF16)
    device_ids = iota((devices, LANES), 0)
    low_ids = iota((LOW, LANES), 0).astype(F32).astype(BF16)
    group_ids = iota((2 * LANES, LANES), 0).astype(F32).astype(BF16)
    acc[...] = jnp.zeros_like(acc)
    one, zero = jnp.ones((), BF16), jnp.zeros((), BF16)

    def step(k, base):
        owners = owner[pl.ds(pl.multiple_of(k * 8, 8), 8), :]
        masks = [jnp.broadcast_to(owners[s : s + 1], (devices, LANES)) == device_ids for s in range(8)]
        hot = jnp.concatenate([jnp.where(m, 1.0, 0.0).astype(BF16) for m in masks], axis=0)
        counted = lax.dot_general(hot, upper, NN, preferred_element_type=F32)
        ranks = []
        for s in range(8):
            part = counted[s * devices : (s + 1) * devices]
            ranks.append(jnp.sum(jnp.where(masks[s], part[:, :LANES] + base, 0.0), axis=0, keepdims=True))
            base = base + part[:, LANES:]
        rank = jnp.concatenate(ranks, axis=0).astype(jnp.int32)
        slot = owners * capacity + rank
        slot_out[pl.ds(pl.multiple_of(k * 8, 8), 8), :] = slot
        low = (slot & (LOW - 1)).astype(F32)
        group = (((slot >> 6) & 1) * LANES + (slot >> 7)).astype(F32)
        for s in range(8):
            lanes = pl.ds(pl.multiple_of(k * 8 * LANES + s * LANES, LANES), LANES)
            hot_low = jnp.where(tiled_rows(low[s : s + 1], LOW) == low_ids, one, zero)
            rhs[s, :, :] = jnp.where(tiled_rows(group[s : s + 1], 2 * LANES) == group_ids, one, zero)
            place = position[:, lanes]
            place = place + jnp.where(iota(place.shape, 0) == 0, 1.0, 0.0)
            for base_row, data in ((0, place), (3, velocity[0:3, lanes])):
                parts = split2(data)
                for c in range(3):
                    for half in range(2):
                        row = (base_row + c) * 2 + half
                        lhs[s, row * LOW : (row + 1) * LOW, :] = hot_low * tiled_rows(parts[half][c : c + 1], LOW)
        left = jnp.concatenate([lhs[s] for s in range(8)], axis=1)
        right = jnp.concatenate([rhs[s] for s in range(8)], axis=1)
        acc[...] += lax.dot_general(left, right, NT, preferred_element_type=F32)
        return base

    lax.fori_loop(0, rows // 8, step, jnp.zeros((devices, LANES), F32))
    for c in range(6):
        both = acc[2 * c * LOW : (2 * c + 1) * LOW, :] + acc[(2 * c + 1) * LOW : (2 * c + 2) * LOW, :]
        square = jnp.concatenate([both[:, :LANES], both[:, LANES:]], axis=0).T
        out[:, c * tiles : (c + 1) * tiles, :] = square.reshape(devices, tiles, LANES)


def face_kernel(center, angle, stiffness, ghost, velocity, slot, own, up, down):
    del slot
    count = stiffness.shape[0]
    faces = count * LANES
    azimuth = angle[0, :].reshape(count, LANES)
    elevation = angle[1, :].reshape(count, LANES)
    flat = jnp.cos(elevation)
    data = [center[c, :].reshape(count, LANES) for c in range(3)]
    data += [jnp.cos(azimuth) * flat, jnp.sin(azimuth) * flat, jnp.sin(elevation), stiffness[...]]
    wanted = ghost[...]
    wanted = jnp.concatenate([wanted, wanted], axis=0)
    row_of, lane_of = wanted >> 7, wanted & (LANES - 1)
    nodes = velocity.shape[1]
    up[...] = jnp.zeros_like(up)
    down[...] = jnp.zeros_like(down)
    up[0:5, :] = velocity[:, nodes - HALO :]
    down[0:5, :] = velocity[:, :HALO]
    for c in range(8):
        if c == 7:
            own[pl.ds(c, count, stride=8), :] = jnp.zeros((count, LANES), F32)
            continue
        own[pl.ds(c, count, stride=8), :] = data[c]
        found = jnp.zeros((8, LANES), F32)
        for r in range(count):
            source = jnp.broadcast_to(data[c][r : r + 1], (8, LANES))
            found = jnp.where(row_of == r, jnp.take_along_axis(source, lane_of, axis=1), found)
        for t in range(2):
            down[8 + 8 * t + c : 9 + 8 * t + c, :] = found[t : t + 1]
            up[8 + 8 * t + c : 9 + 8 * t + c, :] = found[2 + t : 3 + t]


def element_kernel(
    velocity, before, after, connectivity, grads, area, thickness, yields, stress,
    new_stress, spread, token, ext,
):
    nodes = velocity.shape[1]
    rows = nodes // LANES
    pitch = ext.shape[0] // 5
    chunk = 8 * LANES
    for c in range(5):
        ext[c * pitch : c * pitch + 1, :] = before[c : c + 1, :]
        for k in range(rows // 8):
            ext[c * pitch + 1 + 8 * k : c * pitch + 9 + 8 * k, :] = velocity[c, pl.ds(k * chunk, chunk)].reshape(8, LANES)
        ext[c * pitch + rows + 1 : c * pitch + rows + 2, :] = after[c : c + 1, :]
    spread[20 * rows :, :] = jnp.zeros((3 * rows, LANES), F32)
    token[...] = jnp.zeros_like(token)

    def elements(k, carry):
        here = pl.ds(pl.multiple_of(k * chunk, chunk), chunk)
        first = pl.multiple_of(k * 8, 8)
        packed = pl.ds(first, 8)
        sources = [[ext[pl.ds(c * pitch + k * 8 + j, 8), :] for j in range(3)] for c in range(5)]
        row_ids = iota((8, LANES), 0) + k * 8
        corner = []
        for a in range(4):
            index = connectivity[a, here].reshape(8, LANES)
            lane = index & (LANES - 1)
            rel = (index >> 7) - row_ids
            second, third = rel == 1, rel == 2
            values = []
            for c in range(5):
                g = [jnp.take_along_axis(sources[c][j], lane, axis=1) for j in range(3)]
                values.append(jnp.where(third, g[2], jnp.where(second, g[1], g[0])))
            corner.append(values)
        gx = [grads[0, a, here].reshape(8, LANES) for a in range(4)]
        gy = [grads[1, a, here].reshape(8, LANES) for a in range(4)]

        def total(f):
            t = [f(a) for a in range(4)]
            return (t[0] + t[1]) + (t[2] + t[3])

        memb_xx = total(lambda a: gx[a] * corner[a][0])
        bend_xx = total(lambda a: gx[a] * corner[a][4])
        memb_yy = total(lambda a: gy[a] * corner[a][1])
        bend_yy = -total(lambda a: gy[a] * corner[a][3])
        memb_xy = total(lambda a: gy[a] * corner[a][0] + gx[a] * corner[a][1])
        bend_xy = total(lambda a: gy[a] * corner[a][4] - gx[a] * corner[a][3])
        shear_xz = total(lambda a: gx[a] * corner[a][2]) + 0.25 * total(lambda a: corner[a][4])
        shear_yz = total(lambda a: gy[a] * corner[a][2]) - 0.25 * total(lambda a: corner[a][3])
        thick = thickness[packed, :]
        limit = yields[packed, :]
        half_area = 0.5 * thick * area[packed, :]
        force = [None] * 5
        moment = [None] * 3
        for layer in range(5):
            height = (0.5 * LOBATTO_POINTS[layer]) * thick
            xx = memb_xx + height * bend_xx
            yy = memb_yy + height * bend_yy
            xy = memb_xy + height * bend_xy
            old = [stress[layer, c, here].reshape(8, LANES) for c in range(5)]
            t = [
                old[0] + PLANE_MODULUS * (xx + POISSON * yy),
                old[1] + PLANE_MODULUS * (yy + POISSON * xx),
                old[2] + (PLANE_MODULUS * 0.5 * (1.0 - POISSON)) * xy,
                old[3] + SHEAR_MODULUS * shear_xz,
                old[4] + SHEAR_MODULUS * shear_yz,
            ]
            plus, minus = t[0] + t[1], t[0] - t[1]
            mises = jnp.sqrt(
                0.25 * (plus * plus) + 0.75 * (minus * minus) + 3.0 * (t[2] * t[2] + t[3] * t[3] + t[4] * t[4])
            )
            factor = limit / jnp.maximum(mises, limit)
            weight = LOBATTO_WEIGHTS[layer] * half_area
            lever = weight * height
            for c in range(5):
                value = t[c] * factor
                new_stress[layer, c, here] = value.reshape(chunk)
                term = weight * value
                force[c] = term if layer == 0 else force[c] + term
                if c < 3 and layer != 2:
                    term = lever * value
                    moment[c] = term if layer == 0 else moment[c] + term
        for a in range(4):
            out = (
                gx[a] * force[0] + gy[a] * force[2],
                gy[a] * force[1] + gx[a] * force[2],
                gx[a] * force[3] + gy[a] * force[4],
                -(gy[a] * moment[1] + gx[a] * moment[2]) - 0.25 * force[4],
                gx[a] * moment[0] + gy[a] * moment[2] + 0.25 * force[3],
            )
            for c in range(5):
                spread[pl.ds((a * 5 + c) * rows + first, 8), :] = out[c]
        return carry

    lax.fori_loop(0, rows // 8, elements, 0)


def spread_kernel(spread, connectivity, after, own, rim_down, rim_up, acc):
    del after
    rows = connectivity.shape[1] // LANES
    acc[...] = jnp.zeros_like(acc)
    lane_ids = iota((LANES, LANES), 0).astype(F32).astype(BF16)
    one, zero = jnp.ones((), BF16), jnp.zeros((), BF16)

    def scatter_row(b):
        left, right = [], []
        index = connectivity[:, pl.ds(pl.multiple_of(b * LANES, LANES), LANES)]
        lanes = (index & (LANES - 1)).astype(F32)
        rels = ((index >> 7) - b).astype(F32)
        for a in range(4):
            data = spread[pl.ds(a * 5 * rows + b, 8, stride=rows), :]
            high, low = split2(data)
            both = jnp.concatenate([high, low], axis=0).astype(BF16)
            rel = tiled_rows(rels[a : a + 1], 16)
            left.append(jnp.concatenate([jnp.where(rel == jnp.asarray(j, BF16), both, zero) for j in range(3)], axis=0))
            lane = tiled_rows(lanes[a : a + 1], LANES)
            right.append(jnp.where(lane == lane_ids, one, zero))
        out = lax.dot_general(
            jnp.concatenate(left, axis=1), jnp.concatenate(right, axis=1), NT, preferred_element_type=F32
        )
        return [out[16 * j : 16 * j + 8] + out[16 * j + 8 : 16 * j + 16] for j in range(3)]

    def scatter(step, carry):
        b = step * 4
        parts = [scatter_row(b + i) for i in range(4)]
        for i in range(4):
            for j in range(3):
                at = pl.ds(pl.multiple_of((b + i + j) * 8, 8), 8)
                acc[at, :] += parts[i][j]
        return carry

    lax.fori_loop(0, rows // 4, scatter, 0)
    rim_down[...] = acc[0:8, :]
    own[...] = acc[8 : 8 + 8 * rows, :]
    rim_up[...] = acc[8 + 8 * rows : 16 + 8 * rows, :]


def contact_kernel(
    pair_node, pair_face, pair_count, nodes, own, before, after, token, out, raw, face, mean, table, acc, *, devices, tiles
):
    del token
    own_rows = own.shape[0]
    face_tiles = (own_rows + 32) // 8
    raw[0:16, :] = before[8:24, :]
    raw[16 : 16 + own_rows, :] = own[...]
    raw[16 + own_rows :, :] = after[8:24, :]
    sub = iota((8, LANES), 0)

    def prepare(f):
        data = raw[pl.ds(pl.multiple_of(f * 8, 8), 8), :]
        centre = data - 0.5
        normal = [jnp.broadcast_to(data[3 + c : 4 + c], (8, LANES)) for c in range(3)]
        place = [jnp.broadcast_to(centre[c : c + 1], (8, LANES)) for c in range(3)]
        stiff = jnp.broadcast_to(data[6:7], (8, LANES))
        m_low = jnp.where(sub == 0, normal[0], jnp.where(sub == 1, normal[1], jnp.where(sub == 2, normal[2], 0.0)))
        coef_e = jnp.where(sub < 3, (2.0 / REACH_SQ * LOG2E) * centre, jnp.where(sub == 6, 1.0, 0.0))
        coef_d = -m_low
        inside = (sub >= 3) & (sub < 6)
        coef_a = jnp.where(inside, (-DAMPING) * stiff * data, jnp.where(sub == 7, stiff, 0.0))
        square = place[0] * place[0] + place[1] * place[1] + place[2] * place[2]
        along = normal[0] * place[0] + normal[1] * place[1] + normal[2] * place[2]
        for q, (coef, const) in enumerate(((coef_e, (-LOG2E / REACH_SQ) * square), (coef_d, along), (coef_a, None))):
            high, low = split2(coef)
            if const is None:
                last = jnp.where(inside, data, 0.0)
            else:
                c_high, c_low = split2(const)
                last = jnp.where(sub == 0, c_high, jnp.where(sub == 1, c_low, 0.0))
            turned = jnp.concatenate([high, high, low, last], axis=0).T
            packed = turned.astype(BF16)
            for j in range(8):
                at = f * 384 + j * 48
                face[pl.ds(pl.multiple_of(at + q * 16, 16), 16), :] = packed[j * 16 : j * 16 + 16]
                if const is None:
                    for c in range(3):
                        column = turned[j * 16 : j * 16 + 16, 27 + c : 28 + c]
                        mean[pl.ds(pl.multiple_of(at + c * 16, 16), 16), :] = jnp.broadcast_to(column, (16, LANES))

    def prepare_group(i, carry):
        for n in range(4):
            prepare(i * 4 + n)
        return carry

    lax.fori_loop(0, face_tiles // 4, prepare_group, 0)
    total = devices * tiles
    acc[...] = jnp.zeros_like(acc)
    for c in range(6):
        flat = nodes[:, c * tiles : (c + 1) * tiles, :].reshape(total, LANES)
        if c == 0:
            table[pl.ds(7, total, stride=8), :] = jnp.where(flat > 0.5, 1.0, 0.0)
        flat = flat - (1.5, 0.5, 0.5)[c] if c < 3 else flat
        if c < 3:
            square = flat * flat if c == 0 else square + flat * flat
        table[pl.ds(c, total, stride=8), :] = flat
    table[pl.ds(6, total, stride=8), :] = (-LOG2E / REACH_SQ) * square
    ones = jnp.where(sub < 2, 1.0, 0.0)

    def pair_force(node, which):
        high, low = split2(table[pl.ds(pl.multiple_of(node * 8, 8), 8), :])
        matrix = jnp.concatenate([high, low, high, ones], axis=0).astype(BF16)
        at = pl.ds(pl.multiple_of(which * 384, 384), 384)
        terms = lax.dot_general(face[at, :], matrix, NN, preferred_element_type=F32)
        sums = [None] * 3
        for j in range(8):
            power, depth, scale = [terms[j * 48 + q * 16 : j * 48 + q * 16 + 16] for q in range(3)]
            magnitude = jnp.exp2(power) * jnp.maximum(depth, 0.0) * scale
            for c in range(3):
                term = magnitude * mean[pl.ds(pl.multiple_of(which * 384 + j * 48 + c * 16, 16), 16), :]
                term = term[:8] + term[8:]
                sums[c] = term if j == 0 else sums[c] + term
        return sums

    count = pair_count[0]
    group = 8

    def step(i, carry):
        ids = [i * group + n for n in range(group)]
        at = [pair_node[q] for q in ids]
        found = [pair_force(at[n], pair_face[ids[n]]) for n in range(group)]
        for n in range(group):
            keep = jnp.where(ids[n] < count, 1.0, 0.0)
            for c in range(3):
                rows = pl.ds(pl.multiple_of(at[n] * 24 + c * 8, 8), 8)
                acc[rows, :] += found[n][c] * keep
        return carry

    lax.fori_loop(0, (count + group - 1) // group, step, 0)
    for c in range(3):
        value = acc[pl.ds(c * 8, total, stride=24), :]
        for r in range(1, 8):
            value = value + acc[pl.ds(c * 8 + r, total, stride=24), :]
        out[:, c * tiles : (c + 1) * tiles, :] = value.reshape(devices, tiles, LANES)


def final_kernel(back, slot, own, below, above, velocity, inv_mass, out, table, *, tiles):
    devices = back.shape[0]
    rows = slot.shape[0]
    for c in range(3):
        square = back[:, c * tiles : (c + 1) * tiles, :].reshape(devices * tiles, LANES).T
        for half, data in enumerate((square[:LOW], square[LOW:])):
            high, low = split2(data)
            table[half, 2 * c * LOW : (2 * c + 1) * LOW, :] = high.astype(BF16)
            table[half, (2 * c + 1) * LOW : (2 * c + 2) * LOW, :] = low.astype(BF16)
    group_ids = iota((2 * LANES, LANES), 0).astype(F32).astype(BF16)
    low_ids = iota((LOW, LANES), 0)
    one, zero = jnp.ones((), BF16), jnp.zeros((), BF16)
    sub = iota((8, LANES), 0)

    def step(k, carry):
        slots = slot[pl.ds(pl.multiple_of(k * 8, 8), 8), :]
        low = slots & (LOW - 1)
        group = (((slots >> 6) & 1) * LANES + (slots >> 7)).astype(F32)
        for s in range(0, 8, 2):
            hot = [jnp.where(tiled_rows(group[i : i + 1], 2 * LANES) == group_ids, one, zero) for i in (s, s + 1)]
            left = jnp.concatenate([table[0], table[1]], axis=1)
            picked = lax.dot_general(left, jnp.concatenate(hot, axis=1), NN, preferred_element_type=F32)
            for i in range(2):
                r = k * 8 + s + i
                mask = jnp.broadcast_to(low[s + i : s + i + 1], (LOW, LANES)) == low_ids
                contact = jnp.zeros((8, LANES), F32)
                for c in range(3):
                    part = picked[2 * c * LOW : (2 * c + 2) * LOW, i * LANES : (i + 1) * LANES]
                    value = jnp.sum(jnp.where(mask, part[:LOW] + part[LOW:], 0.0), axis=0, keepdims=True)
                    contact = jnp.where(sub == c, value, contact)
                lanes = pl.ds(pl.multiple_of(r * LANES, LANES), LANES)
                total = contact - own[pl.ds(pl.multiple_of(r * 8, 8), 8), :]
                out[:, lanes] = velocity[:, lanes] + inv_mass[pl.ds(r, 1), :] * total[0:5]
        return carry

    lax.fori_loop(0, rows // 8, step, 0)
    last = (rows - 1) * LANES
    out[:, 0:LANES] = out[:, 0:LANES] - inv_mass[0:1, :] * below[0:5, :]
    out[:, last:] = out[:, last:] - inv_mass[rows - 1 : rows, :] * above[0:5, :]


def call(kernel, outs, ins, scratch, cost, smem=0, limit=12):
    vmem = pl.BlockSpec(memory_space=pltpu.VMEM)
    scalar = pl.BlockSpec(memory_space=pltpu.SMEM)
    return pl.pallas_call(
        kernel,
        out_shape=outs,
        in_specs=[scalar] * smem + [vmem] * (len(ins) - smem),
        out_specs=jax.tree.map(lambda _: vmem, outs),
        scratch_shapes=scratch,
        compiler_params=pltpu.CompilerParams(vmem_limit_bytes=limit << 20),
        cost_estimate=pl.CostEstimate(flops=cost, bytes_accessed=cost // 100, transcendentals=0),
    )(*ins)


def body(
    velocity, position, inv_mass, connectivity, shape_grad, area, thickness, yield_stress, stress,
    contact_owner, face_center, face_angle, face_stiffness, ghost_list, pair_node, pair_face, pair_count,
):
    axes = ("dom", "sub")
    devices = lax.axis_size("dom") * lax.axis_size("sub")
    nodes = velocity.shape[1]
    faces = face_center.shape[1]
    rows = nodes // LANES
    capacity = 2 * nodes // devices
    tiles = capacity // LANES
    shape = lambda *s: jax.ShapeDtypeStruct(s, F32)
    view = lambda x: x.reshape(-1, LANES)

    outgoing, slot = call(
        functools.partial(arrange_kernel, devices=devices, capacity=capacity),
        (shape(devices, 6 * tiles, LANES), jax.ShapeDtypeStruct((rows, LANES), jnp.int32)),
        (view(contact_owner), position, velocity),
        [
            pltpu.VMEM((8, 12 * LOW, LANES), BF16),
            pltpu.VMEM((8, 2 * LANES, LANES), BF16),
            pltpu.VMEM((12 * LOW, 2 * LANES), F32),
        ],
        10**9,
        limit=56,
    )
    incoming = lax.all_to_all(outgoing, axes, split_axis=0, concat_axis=0, tiled=True)
    own_faces, send_up, send_down = call(
        face_kernel,
        (shape(faces // LANES * 8, LANES), shape(24, LANES), shape(24, LANES)),
        (face_center, face_angle, view(face_stiffness), view(ghost_list), velocity, slot),
        [],
        10**8,
    )
    up = [(i, i + 1) for i in range(devices - 1)]
    down = [(j, i) for i, j in up]
    before = lax.ppermute(send_up, axes, up)
    after = lax.ppermute(send_down, axes, down)
    new_stress, shares, token = call(
        element_kernel,
        (shape(*stress.shape), shape(23 * rows, LANES), shape(8, LANES)),
        (velocity, before, after, connectivity, shape_grad, view(area), view(thickness), view(yield_stress), stress),
        [pltpu.VMEM((5 * (rows + 8), LANES), F32)],
        10**9,
    )
    face_rows = own_faces.shape[0] + 32
    returned = call(
        functools.partial(contact_kernel, devices=devices, tiles=tiles),
        shape(devices, 3 * tiles, LANES),
        (pair_node, pair_face, pair_count, incoming, own_faces, before, after, token),
        [
            pltpu.VMEM((face_rows, LANES), F32),
            pltpu.VMEM((face_rows * 48, 32), BF16),
            pltpu.VMEM((face_rows * 48, LANES), F32),
            pltpu.VMEM((devices * tiles * 8, LANES), F32),
            pltpu.VMEM((devices * tiles * 24, LANES), F32),
        ],
        10**9,
        smem=3,
    )
    own, rim_down, rim_up = call(
        spread_kernel,
        (shape(8 * rows, LANES), shape(8, LANES), shape(8, LANES)),
        (shares, connectivity, returned),
        [pltpu.VMEM((8 * (rows + 2), LANES), F32)],
        10**9,
    )
    back = lax.all_to_all(returned, axes, split_axis=0, concat_axis=0, tiled=True)
    above = lax.ppermute(rim_down, axes, down)
    below = lax.ppermute(rim_up, axes, up)
    new_velocity = call(
        functools.partial(final_kernel, tiles=tiles),
        shape(*velocity.shape),
        (back, slot, own, below, above, velocity, view(inv_mass)),
        [pltpu.VMEM((2, 6 * LOW, LANES), BF16)],
        10**9,
    )
    return (new_velocity, new_stress)


def solution(mesh):
    split = ("dom", "sub")
    in_specs = (
        P(None, split), P(None, split), P(split), P(None, split), P(None, None, split),
        P(split), P(split), P(split), P(None, None, split), P(split, None),
        P(None, split), P(None, split), P(split), P(split), P(split), P(split), P(split),
    )
    out_specs = (P(None, split), P(None, None, split))
    return jax.shard_map(body, mesh=mesh, in_specs=in_specs, out_specs=out_specs, check_vma=False)
```

```python
import functools

import jax
import jax.numpy as jnp
from jax import lax
from jax.experimental import pallas as pl
from jax.experimental.pallas import tpu as pltpu
from jax.sharding import PartitionSpec as P

LANES = 128
LOW = 64

LOBATTO_POINTS = (-1.0, -0.6546536707079771, 0.0, 0.6546536707079771, 1.0)
LOBATTO_WEIGHTS = (0.1, 49.0 / 90.0, 32.0 / 45.0, 49.0 / 90.0, 0.1)
PLANE_MODULUS = 1.0 / 0.91
POISSON = 0.3
SHEAR_MODULUS = 5.0 / 6.0 / 2.6
DAMPING = 0.3
REACH_SQ = 0.5
LOG2E = 1.4426950408889634

F32 = jnp.float32
BF16 = jnp.bfloat16
NT = (((1,), (1,)), ((), ()))
NN = (((1,), (0,)), ((), ()))


def iota(shape, dim):
    return lax.broadcasted_iota(jnp.int32, shape, dim)


def split2(x):
    high = x.astype(BF16).astype(F32)
    return high, x - high


def tiled_rows(row, count):
    packed = jnp.broadcast_to(row, (16, row.shape[1])).astype(BF16)
    return packed if count == 16 else jnp.concatenate([packed] * (count // 16), axis=0)


def arrange_kernel(owner, position, velocity, out, slot_out, acc, *, devices, capacity):
    rows = owner.shape[0]
    tiles = capacity // LANES
    upper = jnp.where(iota((LANES, 2 * LANES), 1) > iota((LANES, 2 * LANES), 0), 1.0, 0.0).astype(BF16)
    device_ids = iota((devices, LANES), 0)
    low_ids = iota((LOW, LANES), 0).astype(F32).astype(BF16)
    group_ids = iota((2 * LANES, LANES), 0).astype(F32).astype(BF16)
    acc[...] = jnp.zeros_like(acc)
    one, zero = jnp.ones((), BF16), jnp.zeros((), BF16)

    def step(k, base):
        owners = owner[pl.ds(pl.multiple_of(k * 8, 8), 8), :]
        masks = [jnp.broadcast_to(owners[s : s + 1], (devices, LANES)) == device_ids for s in range(8)]
        hot = jnp.concatenate([jnp.where(m, 1.0, 0.0).astype(BF16) for m in masks], axis=0)
        counted = lax.dot_general(hot, upper, NN, preferred_element_type=F32)
        ranks = []
        for s in range(8):
            part = counted[s * devices : (s + 1) * devices]
            ranks.append(jnp.sum(jnp.where(masks[s], part[:, :LANES] + base, 0.0), axis=0, keepdims=True))
            base = base + part[:, LANES:]
        rank = jnp.concatenate(ranks, axis=0).astype(jnp.int32)
        slot = owners * capacity + rank
        slot_out[pl.ds(pl.multiple_of(k * 8, 8), 8), :] = slot
        low = (slot & (LOW - 1)).astype(F32)
        group = (((slot >> 6) & 1) * LANES + (slot >> 7)).astype(F32)
        for first in range(0, 8, 2):
            left, right = [], []
            for s in range(first, first + 2):
                lanes = pl.ds(pl.multiple_of(k * 8 * LANES + s * LANES, LANES), LANES)
                hot_low = jnp.where(tiled_rows(low[s : s + 1], LOW) == low_ids, one, zero)
                right.append(jnp.where(tiled_rows(group[s : s + 1], 2 * LANES) == group_ids, one, zero))
                place = position[:, lanes]
                place = place + jnp.where(iota(place.shape, 0) == 0, 1.0, 0.0)
                column = []
                for data in (place, velocity[0:3, lanes]):
                    parts = split2(data)
                    for c in range(3):
                        for half in range(2):
                            column.append(hot_low * tiled_rows(parts[half][c : c + 1], LOW))
                left.append(jnp.concatenate(column, axis=0))
            acc[...] += lax.dot_general(
                jnp.concatenate(left, axis=1), jnp.concatenate(right, axis=1), NT, preferred_element_type=F32
            )
        return base

    lax.fori_loop(0, rows // 8, step, jnp.zeros((devices, LANES), F32))
    for c in range(6):
        both = acc[2 * c * LOW : (2 * c + 1) * LOW, :] + acc[(2 * c + 1) * LOW : (2 * c + 2) * LOW, :]
        square = jnp.concatenate([both[:, :LANES], both[:, LANES:]], axis=0).T
        out[:, c * tiles : (c + 1) * tiles, :] = square.reshape(devices, tiles, LANES)


FACE_ROWS = 16
PACKET = 72


def packet_kernel(
    center, angle, stiffness, ghost, velocity, stress, grads, connectivity, area, thickness, yields, slot,
    own, up, down, edge_velocity, edge_stress, edge_grads, edge_nodes, edge_scalars, arrived,
):
    del slot
    nodes = velocity.shape[1]
    rows = nodes // LANES
    copies = []
    for side in range(2):
        wide = pl.ds(0, 2 * LANES) if side else pl.ds(nodes - 2 * LANES, 2 * LANES)
        last = pl.ds(0, LANES) if side else pl.ds(nodes - LANES, LANES)
        row = pl.ds(0, 1) if side else pl.ds(rows - 1, 1)
        pairs = [
            (velocity.at[:, wide], edge_velocity.at[side]),
            (stress.at[:, :, last], edge_stress.at[side]),
            (grads.at[:, :, last], edge_grads.at[side]),
            (connectivity.at[:, last], edge_nodes.at[side]),
            (area.at[row], edge_scalars.at[side, 0]),
            (thickness.at[row], edge_scalars.at[side, 1]),
            (yields.at[row], edge_scalars.at[side, 2]),
        ]
        for n, (source, target) in enumerate(pairs):
            copies.append(pltpu.make_async_copy(source, target, arrived.at[side * len(pairs) + n]))
    for copy in copies:
        copy.start()
    count = stiffness.shape[0]
    azimuth = angle[0, :].reshape(count, LANES)
    elevation = angle[1, :].reshape(count, LANES)
    flat = jnp.cos(elevation)
    data = [center[c, :].reshape(count, LANES) for c in range(3)]
    data += [jnp.cos(azimuth) * flat, jnp.sin(azimuth) * flat, jnp.sin(elevation), stiffness[...]]
    wanted = ghost[...]
    wanted = jnp.concatenate([wanted, wanted], axis=0)
    row_of, lane_of = wanted >> 7, wanted & (LANES - 1)
    up[...] = jnp.zeros_like(up)
    down[...] = jnp.zeros_like(down)
    own[pl.ds(7, count, stride=8), :] = jnp.zeros((count, LANES), F32)
    for c in range(7):
        own[pl.ds(c, count, stride=8), :] = data[c]
        found = jnp.zeros((8, LANES), F32)
        for r in range(count):
            source = jnp.broadcast_to(data[c][r : r + 1], (8, LANES))
            found = jnp.where(row_of == r, jnp.take_along_axis(source, lane_of, axis=1), found)
        for t in range(2):
            down[8 * t + c : 8 * t + c + 1, :] = found[t : t + 1]
            up[8 * t + c : 8 * t + c + 1, :] = found[2 + t : 3 + t]
    for copy in copies:
        copy.wait()
    for side, out in ((0, up), (1, down)):
        at = FACE_ROWS
        out[at : at + 5, :] = edge_velocity[side, :, :LANES]
        out[at + 5 : at + 10, :] = edge_velocity[side, :, LANES:]
        at += 10
        for layer in range(5):
            out[at : at + 5, :] = edge_stress[side, layer]
            at += 5
        for g in range(2):
            out[at : at + 4, :] = edge_grads[side, g]
            at += 4
        out[at : at + 4, :] = edge_nodes[side].astype(F32)
        at += 4
        for n in range(3):
            out[at + n : at + n + 1, :] = edge_scalars[side, n]


def element_pack(sources, places, gx, gy, thick, limit, area, old_stress):
    corner = []
    for lane, rel in places:
        second, third = rel == 1, rel == 2
        values = []
        for c in range(5):
            g = [jnp.take_along_axis(sources[c][j], lane, axis=1) for j in range(3)]
            values.append(jnp.where(third, g[2], jnp.where(second, g[1], g[0])))
        corner.append(values)

    def total(f):
        t = [f(a) for a in range(4)]
        return (t[0] + t[1]) + (t[2] + t[3])

    memb_xx = total(lambda a: gx[a] * corner[a][0])
    bend_xx = total(lambda a: gx[a] * corner[a][4])
    memb_yy = total(lambda a: gy[a] * corner[a][1])
    bend_yy = -total(lambda a: gy[a] * corner[a][3])
    memb_xy = total(lambda a: gy[a] * corner[a][0] + gx[a] * corner[a][1])
    bend_xy = total(lambda a: gy[a] * corner[a][4] - gx[a] * corner[a][3])
    shear_xz = total(lambda a: gx[a] * corner[a][2]) + 0.25 * total(lambda a: corner[a][4])
    shear_yz = total(lambda a: gy[a] * corner[a][2]) - 0.25 * total(lambda a: corner[a][3])
    half_area = 0.5 * thick * area
    force = [None] * 5
    moment = [None] * 3
    stresses = []
    for layer in range(5):
        height = (0.5 * LOBATTO_POINTS[layer]) * thick
        xx = memb_xx + height * bend_xx
        yy = memb_yy + height * bend_yy
        xy = memb_xy + height * bend_xy
        old = old_stress(layer)
        t = [
            old[0] + PLANE_MODULUS * (xx + POISSON * yy),
            old[1] + PLANE_MODULUS * (yy + POISSON * xx),
            old[2] + (PLANE_MODULUS * 0.5 * (1.0 - POISSON)) * xy,
            old[3] + SHEAR_MODULUS * shear_xz,
            old[4] + SHEAR_MODULUS * shear_yz,
        ]
        plus, minus = t[0] + t[1], t[0] - t[1]
        mises = jnp.sqrt(
            0.25 * (plus * plus) + 0.75 * (minus * minus) + 3.0 * (t[2] * t[2] + t[3] * t[3] + t[4] * t[4])
        )
        factor = limit / jnp.maximum(mises, limit)
        weight = LOBATTO_WEIGHTS[layer] * half_area
        lever = weight * height
        values = [t[c] * factor for c in range(5)]
        stresses.append(values)
        for c in range(5):
            term = weight * values[c]
            force[c] = term if layer == 0 else force[c] + term
            if c < 3 and layer != 2:
                term = lever * values[c]
                moment[c] = term if layer == 0 else moment[c] + term
    forces = [
        (
            gx[a] * force[0] + gy[a] * force[2],
            gy[a] * force[1] + gx[a] * force[2],
            gx[a] * force[3] + gy[a] * force[4],
            -(gy[a] * moment[1] + gx[a] * moment[2]) - 0.25 * force[4],
            gx[a] * moment[0] + gy[a] * moment[2] + 0.25 * force[3],
        )
        for a in range(4)
    ]
    return forces, stresses


def spread_row(spread, pitch, row, lanes, rels, wanted):
    one, zero = jnp.ones((), BF16), jnp.zeros((), BF16)
    lane_ids = iota((LANES, LANES), 0).astype(F32).astype(BF16)
    left, right = [], []
    for a in range(4):
        data = spread[pl.ds(a * 5 * pitch + row, 8, stride=pitch), :]
        high, low = split2(data)
        both = jnp.concatenate([high, low], axis=0).astype(BF16)
        rel = tiled_rows(rels[a : a + 1], 16)
        left.append(jnp.concatenate([jnp.where(rel == jnp.asarray(j, BF16), both, zero) for j in wanted], axis=0))
        lane = tiled_rows(lanes[a : a + 1], LANES)
        right.append(jnp.where(lane == lane_ids, one, zero))
    out = lax.dot_general(
        jnp.concatenate(left, axis=1), jnp.concatenate(right, axis=1), NT, preferred_element_type=F32
    )
    return [out[16 * j : 16 * j + 8] + out[16 * j + 8 : 16 * j + 16] for j in range(len(wanted))]


def element_kernel(
    velocity, before, after, connectivity, grads, area, thickness, yields, stress, returned,
    new_stress, own, ext, spread, acc,
):
    del returned
    nodes = velocity.shape[1]
    rows = nodes // LANES
    pitch = rows + 8
    chunk = 8 * LANES
    for c in range(5):
        at = FACE_ROWS + c
        ext[c * pitch : c * pitch + 1, :] = before[at : at + 1, :]
        ext[c * pitch + 1 : c * pitch + 2, :] = before[at + 5 : at + 6, :]
        for k in range(rows // 8):
            ext[c * pitch + 2 + 8 * k : c * pitch + 10 + 8 * k, :] = velocity[c, pl.ds(k * chunk, chunk)].reshape(8, LANES)
        ext[c * pitch + rows + 2 : c * pitch + rows + 3, :] = after[at : at + 1, :]
        ext[c * pitch + rows + 3 : c * pitch + rows + 4, :] = after[at + 5 : at + 6, :]
    spread[20 * pitch :, :] = jnp.zeros((3 * pitch, LANES), F32)

    def elements(k, carry):
        here = pl.ds(pl.multiple_of(k * chunk, chunk), chunk)
        first = pl.multiple_of(k * 8, 8)
        packed = pl.ds(first, 8)
        sources = [[ext[pl.ds(c * pitch + k * 8 + j + 1, 8), :] for j in range(3)] for c in range(5)]
        row_ids = iota((8, LANES), 0) + k * 8
        places = []
        for a in range(4):
            index = connectivity[a, here].reshape(8, LANES)
            places.append((index & (LANES - 1), (index >> 7) - row_ids))
        gx = [grads[0, a, here].reshape(8, LANES) for a in range(4)]
        gy = [grads[1, a, here].reshape(8, LANES) for a in range(4)]
        forces, stresses = element_pack(
            sources, places, gx, gy, thickness[packed, :], yields[packed, :], area[packed, :],
            lambda layer: [stress[layer, c, here].reshape(8, LANES) for c in range(5)],
        )
        for layer in range(5):
            for c in range(5):
                new_stress[layer, c, here] = stresses[layer][c].reshape(chunk)
        for a in range(4):
            for c in range(5):
                spread[pl.ds((a * 5 + c) * pitch + first, 8), :] = forces[a][c]
        return carry

    lax.fori_loop(0, rows // 8, elements, 0)
    blank = jnp.zeros((6, LANES), F32)

    def edge(n):
        at = FACE_ROWS + 10 + n
        return jnp.concatenate([before[at : at + 1, :], after[at : at + 1, :], blank], axis=0)

    sub = iota((8, LANES), 0)
    sources = [
        [
            jnp.concatenate(
                [ext[c * pitch + j : c * pitch + j + 1, :], ext[c * pitch + rows + 1 + j : c * pitch + rows + 2 + j, :], blank],
                axis=0,
            )
            for j in range(3)
        ]
        for c in range(5)
    ]
    places = []
    for a in range(4):
        index = edge(33 + a).astype(jnp.int32) + jnp.where(sub == 0, -nodes, nodes)
        places.append((index & (LANES - 1), jnp.where(sub == 0, (index >> 7) + 1, (index >> 7) - rows)))
    limit = edge(39)
    forces, _ = element_pack(
        sources, places, [edge(25 + a) for a in range(4)], [edge(29 + a) for a in range(4)],
        edge(38), jnp.where(limit > 0.0, limit, 1.0), edge(37),
        lambda layer: [edge(layer * 5 + c) for c in range(5)],
    )
    for a in range(4):
        for c in range(5):
            at = (a * 5 + c) * pitch + rows
            spread[at : at + 8, :] = forces[a][c]

    acc[...] = jnp.zeros_like(acc)

    def scatter(step, carry):
        b = step * 4
        parts = []
        for i in range(4):
            index = connectivity[:, pl.ds(pl.multiple_of((b + i) * LANES, LANES), LANES)]
            lanes = (index & (LANES - 1)).astype(F32)
            rels = ((index >> 7) - (b + i)).astype(F32)
            parts.append(spread_row(spread, pitch, b + i, lanes, rels, (0, 1, 2)))
        total = {}
        for i in range(4):
            for j in range(3):
                total[i + j] = parts[i][j] if i + j not in total else total[i + j] + parts[i][j]
        for n in range(6):
            at = pl.ds(pl.multiple_of((b + n) * 8, 8), 8)
            if n < 2:
                acc[at, :] += total[n]
            else:
                acc[at, :] = total[n]
        return carry

    lax.fori_loop(0, rows // 4, scatter, 0)
    for side, row, j in ((0, 1, 2), (1, rows, 0)):
        lanes = jnp.concatenate([place[0][side : side + 1] for place in places], axis=0).astype(F32)
        rels = jnp.concatenate([place[1][side : side + 1] for place in places], axis=0).astype(F32)
        acc[8 * row : 8 * row + 8, :] += spread_row(spread, pitch, rows + side, lanes, rels, (j,))[0]
    own[...] = acc[8 : 8 + 8 * rows, :]


def contact_kernel(
    pair_node, pair_face, pair_count, nodes, own, before, after, out, raw, face, mean, table, acc, *, devices, tiles
):
    own_rows = own.shape[0]
    face_tiles = (own_rows + 32) // 8
    raw[0:16, :] = before[0:FACE_ROWS, :]
    raw[16 : 16 + own_rows, :] = own[...]
    raw[16 + own_rows :, :] = after[0:FACE_ROWS, :]
    sub = iota((8, LANES), 0)

    def prepare(f):
        data = raw[pl.ds(pl.multiple_of(f * 8, 8), 8), :]
        centre = data - 0.5
        normal = [jnp.broadcast_to(data[3 + c : 4 + c], (8, LANES)) for c in range(3)]
        place = [jnp.broadcast_to(centre[c : c + 1], (8, LANES)) for c in range(3)]
        stiff = jnp.broadcast_to(data[6:7], (8, LANES))
        m_low = jnp.where(sub == 0, normal[0], jnp.where(sub == 1, normal[1], jnp.where(sub == 2, normal[2], 0.0)))
        coef_e = jnp.where(sub < 3, (2.0 / REACH_SQ * LOG2E) * centre, jnp.where(sub == 6, 1.0, 0.0))
        coef_d = -m_low
        inside = (sub >= 3) & (sub < 6)
        coef_a = jnp.where(inside, (-DAMPING) * stiff * data, jnp.where(sub == 7, stiff, 0.0))
        square = place[0] * place[0] + place[1] * place[1] + place[2] * place[2]
        along = normal[0] * place[0] + normal[1] * place[1] + normal[2] * place[2]
        for q, (coef, const) in enumerate(((coef_e, (-LOG2E / REACH_SQ) * square), (coef_d, along), (coef_a, None))):
            high, low = split2(coef)
            if const is None:
                last = jnp.where(inside, data, 0.0)
            else:
                c_high, c_low = split2(const)
                last = jnp.where(sub == 0, c_high, jnp.where(sub == 1, c_low, 0.0))
            turned = jnp.concatenate([high, high, low, last], axis=0).T
            packed = turned.astype(BF16)
            for j in range(8):
                at = f * 384 + j * 48
                face[pl.ds(pl.multiple_of(at + q * 16, 16), 16), :] = packed[j * 16 : j * 16 + 16]
                if const is None:
                    for c in range(3):
                        column = turned[j * 16 : j * 16 + 16, 27 + c : 28 + c]
                        mean[pl.ds(pl.multiple_of(at + c * 16, 16), 16), :] = jnp.broadcast_to(column, (16, LANES))

    def prepare_group(i, carry):
        for n in range(4):
            prepare(i * 4 + n)
        return carry

    lax.fori_loop(0, face_tiles // 4, prepare_group, 0)
    total = devices * tiles
    acc[...] = jnp.zeros_like(acc)
    for c in range(6):
        flat = nodes[:, c * tiles : (c + 1) * tiles, :].reshape(total, LANES)
        if c == 0:
            table[pl.ds(7, total, stride=8), :] = jnp.where(flat > 0.5, 1.0, 0.0)
        flat = flat - (1.5, 0.5, 0.5)[c] if c < 3 else flat
        if c < 3:
            square = flat * flat if c == 0 else square + flat * flat
        table[pl.ds(c, total, stride=8), :] = flat
    table[pl.ds(6, total, stride=8), :] = (-LOG2E / REACH_SQ) * square
    ones = jnp.where(sub < 2, 1.0, 0.0)

    def pair_force(node, which):
        high, low = split2(table[pl.ds(pl.multiple_of(node * 8, 8), 8), :])
        matrix = jnp.concatenate([high, low, high, ones], axis=0).astype(BF16)
        at = pl.ds(pl.multiple_of(which * 384, 384), 384)
        terms = lax.dot_general(face[at, :], matrix, NN, preferred_element_type=F32)
        sums = [None] * 3
        for j in range(8):
            power, depth, scale = [terms[j * 48 + q * 16 : j * 48 + q * 16 + 16] for q in range(3)]
            magnitude = jnp.exp2(power) * jnp.maximum(depth, 0.0) * scale
            for c in range(3):
                term = magnitude * mean[pl.ds(pl.multiple_of(which * 384 + j * 48 + c * 16, 16), 16), :]
                term = term[:8] + term[8:]
                sums[c] = term if j == 0 else sums[c] + term
        return sums

    count = pair_count[0]
    group = 8

    def step(i, carry):
        ids = [i * group + n for n in range(group)]
        at = [pair_node[q] for q in ids]
        found = [pair_force(at[n], pair_face[ids[n]]) for n in range(group)]
        for n in range(group):
            keep = jnp.where(ids[n] < count, 1.0, 0.0)
            for c in range(3):
                rows = pl.ds(pl.multiple_of(at[n] * 24 + c * 8, 8), 8)
                acc[rows, :] += found[n][c] * keep
        return carry

    lax.fori_loop(0, (count + group - 1) // group, step, 0)
    for c in range(3):
        value = acc[pl.ds(c * 8, total, stride=24), :]
        for r in range(1, 8):
            value = value + acc[pl.ds(c * 8 + r, total, stride=24), :]
        out[:, c * tiles : (c + 1) * tiles, :] = value.reshape(devices, tiles, LANES)


def final_kernel(back, slot, own, velocity, inv_mass, out, table, *, tiles):
    devices = back.shape[0]
    rows = slot.shape[0]
    for c in range(3):
        square = back[:, c * tiles : (c + 1) * tiles, :].reshape(devices * tiles, LANES).T
        for half, data in enumerate((square[:LOW], square[LOW:])):
            high, low = split2(data)
            table[half, 2 * c * LOW : (2 * c + 1) * LOW, :] = high.astype(BF16)
            table[half, (2 * c + 1) * LOW : (2 * c + 2) * LOW, :] = low.astype(BF16)
    group_ids = iota((2 * LANES, LANES), 0).astype(F32).astype(BF16)
    low_ids = iota((LOW, LANES), 0)
    one, zero = jnp.ones((), BF16), jnp.zeros((), BF16)
    sub = iota((8, LANES), 0)

    def step(k, carry):
        slots = slot[pl.ds(pl.multiple_of(k * 8, 8), 8), :]
        low = slots & (LOW - 1)
        group = (((slots >> 6) & 1) * LANES + (slots >> 7)).astype(F32)
        for s in range(0, 8, 2):
            hot = [jnp.where(tiled_rows(group[i : i + 1], 2 * LANES) == group_ids, one, zero) for i in (s, s + 1)]
            left = jnp.concatenate([table[0], table[1]], axis=1)
            picked = lax.dot_general(left, jnp.concatenate(hot, axis=1), NN, preferred_element_type=F32)
            for i in range(2):
                r = k * 8 + s + i
                mask = jnp.broadcast_to(low[s + i : s + i + 1], (LOW, LANES)) == low_ids
                contact = jnp.zeros((8, LANES), F32)
                for c in range(3):
                    part = picked[2 * c * LOW : (2 * c + 2) * LOW, i * LANES : (i + 1) * LANES]
                    value = jnp.sum(jnp.where(mask, part[:LOW] + part[LOW:], 0.0), axis=0, keepdims=True)
                    contact = jnp.where(sub == c, value, contact)
                lanes = pl.ds(pl.multiple_of(r * LANES, LANES), LANES)
                total = contact - own[pl.ds(pl.multiple_of(r * 8, 8), 8), :]
                out[:, lanes] = velocity[:, lanes] + inv_mass[pl.ds(r, 1), :] * total[0:5]
        return carry

    lax.fori_loop(0, rows // 8, step, 0)


def call(kernel, outs, ins, scratch, cost, smem=0, limit=12, away=()):
    vmem = pl.BlockSpec(memory_space=pltpu.VMEM)
    scalar = pl.BlockSpec(memory_space=pltpu.SMEM)
    return pl.pallas_call(
        kernel,
        out_shape=outs,
        in_specs=[scalar if n < smem else pl.BlockSpec(memory_space=pl.ANY) if n in away else vmem for n in range(len(ins))],
        out_specs=jax.tree.map(lambda _: vmem, outs),
        scratch_shapes=scratch,
        compiler_params=pltpu.CompilerParams(vmem_limit_bytes=limit << 20),
        cost_estimate=pl.CostEstimate(flops=cost, bytes_accessed=cost // 100, transcendentals=0),
    )(*ins)


def body(
    velocity, position, inv_mass, connectivity, shape_grad, area, thickness, yield_stress, stress,
    contact_owner, face_center, face_angle, face_stiffness, ghost_list, pair_node, pair_face, pair_count,
):
    axes = ("dom", "sub")
    devices = lax.axis_size("dom") * lax.axis_size("sub")
    nodes = velocity.shape[1]
    faces = face_center.shape[1]
    rows = nodes // LANES
    capacity = 2 * nodes // devices
    tiles = capacity // LANES
    shape = lambda *s: jax.ShapeDtypeStruct(s, F32)
    view = lambda x: x.reshape(-1, LANES)

    outgoing, slot = call(
        functools.partial(arrange_kernel, devices=devices, capacity=capacity),
        (shape(devices, 6 * tiles, LANES), jax.ShapeDtypeStruct((rows, LANES), jnp.int32)),
        (view(contact_owner), position, velocity),
        [
            pltpu.VMEM((12 * LOW, 2 * LANES), F32),
        ],
        10**9,
        limit=56,
    )
    incoming = lax.all_to_all(outgoing, axes, split_axis=0, concat_axis=0, tiled=True)
    own_faces, send_up, send_down = call(
        packet_kernel,
        (shape(faces // LANES * 8, LANES), shape(PACKET, LANES), shape(PACKET, LANES)),
        (
            face_center, face_angle, view(face_stiffness), view(ghost_list), velocity, stress, shape_grad,
            connectivity, view(area), view(thickness), view(yield_stress), slot,
        ),
        [
            pltpu.VMEM((2, 5, 2 * LANES), F32),
            pltpu.VMEM((2, 5, 5, LANES), F32),
            pltpu.VMEM((2, 2, 4, LANES), F32),
            pltpu.VMEM((2, 4, LANES), jnp.int32),
            pltpu.VMEM((2, 3, 1, LANES), F32),
            pltpu.SemaphoreType.DMA((14,)),
        ],
        10**8,
        away=range(4, 12),
    )
    up = [(i, i + 1) for i in range(devices - 1)]
    down = [(j, i) for i, j in up]
    before = lax.ppermute(send_up, axes, up)
    after = lax.ppermute(send_down, axes, down)
    face_rows = own_faces.shape[0] + 32
    returned = call(
        functools.partial(contact_kernel, devices=devices, tiles=tiles),
        shape(devices, 3 * tiles, LANES),
        (pair_node, pair_face, pair_count, incoming, own_faces, before, after),
        [
            pltpu.VMEM((face_rows, LANES), F32),
            pltpu.VMEM((face_rows * 48, 32), BF16),
            pltpu.VMEM((face_rows * 48, LANES), F32),
            pltpu.VMEM((devices * tiles * 8, LANES), F32),
            pltpu.VMEM((devices * tiles * 24, LANES), F32),
        ],
        10**9,
        smem=3,
    )
    back = lax.all_to_all(returned, axes, split_axis=0, concat_axis=0, tiled=True)
    new_stress, own = call(
        element_kernel,
        (shape(*stress.shape), shape(8 * rows, LANES)),
        (
            velocity, before, after, connectivity, shape_grad, view(area), view(thickness), view(yield_stress),
            stress, returned,
        ),
        [
            pltpu.VMEM((5 * (rows + 8), LANES), F32),
            pltpu.VMEM((23 * (rows + 8), LANES), F32),
            pltpu.VMEM((8 * (rows + 2), LANES), F32),
        ],
        10**9,
        away=(9,),
    )
    new_velocity = call(
        functools.partial(final_kernel, tiles=tiles),
        shape(*velocity.shape),
        (back, slot, own, velocity, view(inv_mass)),
        [pltpu.VMEM((2, 6 * LOW, LANES), BF16)],
        10**9,
    )
    return (new_velocity, new_stress)


def solution(mesh):
    split = ("dom", "sub")
    in_specs = (
        P(None, split), P(None, split), P(split), P(None, split), P(None, None, split),
        P(split), P(split), P(split), P(None, None, split), P(split, None),
        P(None, split), P(None, split), P(split), P(split), P(split), P(split), P(split),
    )
    out_specs = (P(None, split), P(None, None, split))
    return jax.shard_map(body, mesh=mesh, in_specs=in_specs, out_specs=out_specs, check_vma=False)
```

```python
import functools
import math

import jax
import jax.numpy as jnp
from jax import lax
from jax.experimental import pallas as pl
from jax.experimental.pallas import tpu as pltpu
from jax.sharding import PartitionSpec as P

LANES = 128
LOW = 64
THIN = 32

LOBATTO_POINTS = (-1.0, -0.6546536707079771, 0.0, 0.6546536707079771, 1.0)
LOBATTO_WEIGHTS = (0.1, 49.0 / 90.0, 32.0 / 45.0, 49.0 / 90.0, 0.1)
PLANE_MODULUS = 1.0 / 0.91
POISSON = 0.3
SHEAR_MODULUS = 5.0 / 6.0 / 2.6
DAMPING = 0.3
REACH_SQ = 0.5
LOG2E = 1.4426950408889634

F32 = jnp.float32
BF16 = jnp.bfloat16
NT = (((1,), (1,)), ((), ()))
NN = (((1,), (0,)), ((), ()))


def iota(shape, dim):
    return lax.broadcasted_iota(jnp.int32, shape, dim)


def split2(x):
    high = x.astype(BF16).astype(F32)
    return high, x - high


def tiled_rows(row, count):
    packed = jnp.broadcast_to(row, (16, row.shape[1])).astype(BF16)
    return packed if count == 16 else jnp.concatenate([packed] * (count // 16), axis=0)


def arrange_kernel(
    owner, position_away, velocity_away, out, slot_out, acc, ordered, bounds, bounds_scalar, position, velocity,
    arrived, *, devices, capacity
):
    rows = owner.shape[0]
    load_position = pltpu.make_async_copy(position_away, position, arrived.at[1])
    load_velocity = pltpu.make_async_copy(velocity_away, velocity, arrived.at[2])
    load_position.start()
    load_velocity.start()
    tiles = capacity // LANES
    upper = jnp.where(iota((LANES, 2 * LANES), 1) > iota((LANES, 2 * LANES), 0), 1.0, 0.0).astype(BF16)
    device_ids = iota((devices, LANES), 0)

    def count(k, base):
        owners = owner[pl.ds(pl.multiple_of(k * 32, 32), 32), :]
        masks = [jnp.broadcast_to(owners[s : s + 1], (devices, LANES)) == device_ids for s in range(32)]
        hot = jnp.concatenate([jnp.where(m, 1.0, 0.0).astype(BF16) for m in masks], axis=0)
        counted = lax.dot_general(hot, upper, NN, preferred_element_type=F32)
        ranks = []
        for s in range(32):
            part = counted[s * devices : (s + 1) * devices]
            ranks.append(jnp.sum(jnp.where(masks[s], part[:, :LANES] + base, 0.0), axis=0, keepdims=True))
            base = base + part[:, LANES:]
        rank = jnp.concatenate(ranks, axis=0).astype(jnp.int32)
        slot_out[pl.ds(pl.multiple_of(k * 32, 32), 32), :] = owners * capacity + rank
        return base

    totals = lax.fori_loop(0, rows // 32, count, jnp.zeros((devices, LANES), F32))
    lower = jnp.where(iota((devices, devices), 0) > iota((devices, devices), 1), 1.0, 0.0).astype(BF16)
    high, low = split2(totals)
    starts = lax.dot_general(lower, jnp.concatenate([high, low], axis=1).astype(BF16), NN, preferred_element_type=F32)
    starts = starts[:, :LANES] + starts[:, LANES:]
    by_lane = []
    for data in (starts, totals):
        if devices < LANES:
            data = jnp.concatenate([data, jnp.zeros((LANES - devices, LANES), F32)], axis=0)
        by_lane.append(data.T[0:8].astype(jnp.int32))
    start_lanes = by_lane[0]
    bounds[...] = jnp.where(iota((8, LANES), 0) == 0, by_lane[0], by_lane[1])
    copy = pltpu.make_async_copy(bounds, bounds_scalar, arrived.at[0])
    copy.start()

    low_ids = iota((THIN, LANES), 0).astype(F32).astype(BF16)
    group_ids = iota((2 * LANES, LANES), 0).astype(F32).astype(BF16)
    acc[...] = jnp.zeros_like(acc)
    one, zero = jnp.ones((), BF16), jnp.zeros((), BF16)
    load_position.wait()
    load_velocity.wait()

    def sort(k, carry):
        owners = owner[pl.ds(pl.multiple_of(k * 64, 64), 64), :]
        rank = slot_out[pl.ds(pl.multiple_of(k * 64, 64), 64), :] - owners * capacity
        place = jnp.concatenate([jnp.take_along_axis(start_lanes, owners[8 * h : 8 * h + 8], axis=1) for h in range(8)], axis=0) + rank
        low = (place & (THIN - 1)).astype(F32)
        group = (((place >> 6) & 1) * LANES + ((place >> 5) & 1) * (LANES // 2) + (place >> 7)).astype(F32)
        left, right = [], []
        for s in range(64):
            lanes = pl.ds(pl.multiple_of(k * 64 * LANES + s * LANES, LANES), LANES)
            hot_low = jnp.where(tiled_rows(low[s : s + 1], THIN) == low_ids, one, zero)
            right.append(jnp.where(tiled_rows(group[s : s + 1], 2 * LANES) == group_ids, one, zero))
            where = position[:, lanes]
            where = where + jnp.where(iota(where.shape, 0) == 0, 1.0, 0.0)
            column = []
            for data in (where, velocity[0:3, lanes]):
                parts = split2(data)
                for c in range(3):
                    for half in range(2):
                        column.append(hot_low * tiled_rows(parts[half][c : c + 1], THIN))
            left.append(jnp.concatenate(column, axis=0))
        acc[...] += lax.dot_general(
            jnp.concatenate(left, axis=1), jnp.concatenate(right, axis=1), NT, preferred_element_type=F32
        )
        return carry

    lax.fori_loop(0, rows // 64, sort, 0)
    for c in range(6):
        both = acc[2 * c * THIN : (2 * c + 1) * THIN, :] + acc[(2 * c + 1) * THIN : (2 * c + 2) * THIN, :]
        pieces = []
        for data in (both[:, :LANES], both[:, LANES:]):
            pieces += [data, pltpu.roll(data, LANES // 2, 1)]
        ordered[pl.ds(c, rows, stride=8), :] = jnp.concatenate(pieces, axis=0).T[0:rows]
    ordered[8 * rows :, :] = jnp.zeros((8, LANES), F32)
    copy.wait()
    lane = iota((8, LANES), 1)

    def place_runs(i, carry):
        for n in range(4):
            device = i * 4 + n
            start, amount = bounds_scalar[0, device], bounds_scalar[1, device]
            for t in range(tiles):
                at = start + t * LANES
                row = jnp.minimum(at >> 7, rows - 1)
                shift = at & (LANES - 1)
                this = ordered[pl.ds(pl.multiple_of(row * 8, 8), 8), :]
                following = ordered[pl.ds(pl.multiple_of(row * 8 + 8, 8), 8), :]
                turned = pltpu.roll(jnp.where(lane >= shift, this, following), (LANES - shift) & (LANES - 1), 1)
                out[device, pl.ds(t, 6, stride=tiles), :] = jnp.where(lane < amount - t * LANES, turned, 0.0)[0:6]
        return carry

    lax.fori_loop(0, devices // 4, place_runs, 0)


FACE_ROWS = 16
PACKET = 72


def packet_kernel(
    center, angle, stiffness, ghost, velocity, stress, grads, connectivity, area, thickness, yields, slot,
    own, up, down, edge_velocity, edge_stress, edge_grads, edge_nodes, edge_scalars, arrived,
):
    del slot
    nodes = velocity.shape[1]
    rows = nodes // LANES
    copies = []
    for side in range(2):
        wide = pl.ds(0, 2 * LANES) if side else pl.ds(nodes - 2 * LANES, 2 * LANES)
        last = pl.ds(0, LANES) if side else pl.ds(nodes - LANES, LANES)
        row = pl.ds(0, 1) if side else pl.ds(rows - 1, 1)
        pairs = [
            (velocity.at[:, wide], edge_velocity.at[side]),
            (stress.at[:, :, last], edge_stress.at[side]),
            (grads.at[:, :, last], edge_grads.at[side]),
            (connectivity.at[:, last], edge_nodes.at[side]),
            (area.at[row], edge_scalars.at[side, 0]),
            (thickness.at[row], edge_scalars.at[side, 1]),
            (yields.at[row], edge_scalars.at[side, 2]),
        ]
        for n, (source, target) in enumerate(pairs):
            copies.append(pltpu.make_async_copy(source, target, arrived.at[side * len(pairs) + n]))
    for copy in copies:
        copy.start()
    count = stiffness.shape[0]
    azimuth = angle[0, :].reshape(count, LANES)
    elevation = angle[1, :].reshape(count, LANES)
    flat = jnp.cos(elevation)
    data = [center[c, :].reshape(count, LANES) for c in range(3)]
    data += [jnp.cos(azimuth) * flat, jnp.sin(azimuth) * flat, jnp.sin(elevation), stiffness[...]]
    wanted = ghost[...]
    wanted = jnp.concatenate([wanted, wanted], axis=0)
    row_of, lane_of = wanted >> 7, wanted & (LANES - 1)
    up[...] = jnp.zeros_like(up)
    down[...] = jnp.zeros_like(down)
    own[pl.ds(7, count, stride=8), :] = jnp.zeros((count, LANES), F32)
    for c in range(7):
        own[pl.ds(c, count, stride=8), :] = data[c]
        found = jnp.zeros((8, LANES), F32)
        for r in range(count):
            source = jnp.broadcast_to(data[c][r : r + 1], (8, LANES))
            found = jnp.where(row_of == r, jnp.take_along_axis(source, lane_of, axis=1), found)
        for t in range(2):
            down[8 * t + c : 8 * t + c + 1, :] = found[t : t + 1]
            up[8 * t + c : 8 * t + c + 1, :] = found[2 + t : 3 + t]
    for copy in copies:
        copy.wait()
    for side, out in ((0, up), (1, down)):
        at = FACE_ROWS
        out[at : at + 5, :] = edge_velocity[side, :, :LANES]
        out[at + 5 : at + 10, :] = edge_velocity[side, :, LANES:]
        at += 10
        for layer in range(5):
            out[at : at + 5, :] = edge_stress[side, layer]
            at += 5
        for g in range(2):
            out[at : at + 4, :] = edge_grads[side, g]
            at += 4
        out[at : at + 4, :] = edge_nodes[side].astype(F32)
        at += 4
        for n in range(3):
            out[at + n : at + n + 1, :] = edge_scalars[side, n]


def element_pack(sources, places, gx, gy, thick, limit, area, old_stress):
    corner = []
    for lane, rel in places:
        second, third = rel == 1, rel == 2
        values = []
        for c in range(5):
            g = [jnp.take_along_axis(sources[c][j], lane, axis=1) for j in range(3)]
            values.append(jnp.where(third, g[2], jnp.where(second, g[1], g[0])))
        corner.append(values)

    def total(f):
        t = [f(a) for a in range(4)]
        return (t[0] + t[1]) + (t[2] + t[3])

    memb_xx = total(lambda a: gx[a] * corner[a][0])
    bend_xx = total(lambda a: gx[a] * corner[a][4])
    memb_yy = total(lambda a: gy[a] * corner[a][1])
    bend_yy = -total(lambda a: gy[a] * corner[a][3])
    memb_xy = total(lambda a: gy[a] * corner[a][0] + gx[a] * corner[a][1])
    bend_xy = total(lambda a: gy[a] * corner[a][4] - gx[a] * corner[a][3])
    shear_xz = total(lambda a: gx[a] * corner[a][2]) + 0.25 * total(lambda a: corner[a][4])
    shear_yz = total(lambda a: gy[a] * corner[a][2]) - 0.25 * total(lambda a: corner[a][3])
    half_area = 0.5 * thick * area
    force = [None] * 5
    moment = [None] * 3
    stresses = []
    for layer in range(5):
        height = (0.5 * LOBATTO_POINTS[layer]) * thick
        xx = memb_xx + height * bend_xx
        yy = memb_yy + height * bend_yy
        xy = memb_xy + height * bend_xy
        old = old_stress(layer)
        t = [
            old[0] + PLANE_MODULUS * (xx + POISSON * yy),
            old[1] + PLANE_MODULUS * (yy + POISSON * xx),
            old[2] + (PLANE_MODULUS * 0.5 * (1.0 - POISSON)) * xy,
            old[3] + SHEAR_MODULUS * shear_xz,
            old[4] + SHEAR_MODULUS * shear_yz,
        ]
        plus, minus = t[0] + t[1], t[0] - t[1]
        mises = jnp.sqrt(
            0.25 * (plus * plus) + 0.75 * (minus * minus) + 3.0 * (t[2] * t[2] + t[3] * t[3] + t[4] * t[4])
        )
        factor = limit / jnp.maximum(mises, limit)
        weight = LOBATTO_WEIGHTS[layer] * half_area
        lever = weight * height
        values = [t[c] * factor for c in range(5)]
        stresses.append(values)
        for c in range(5):
            term = weight * values[c]
            force[c] = term if layer == 0 else force[c] + term
            if c < 3 and layer != 2:
                term = lever * values[c]
                moment[c] = term if layer == 0 else moment[c] + term
    forces = [
        (
            gx[a] * force[0] + gy[a] * force[2],
            gy[a] * force[1] + gx[a] * force[2],
            gx[a] * force[3] + gy[a] * force[4],
            -(gy[a] * moment[1] + gx[a] * moment[2]) - 0.25 * force[4],
            gx[a] * moment[0] + gy[a] * moment[2] + 0.25 * force[3],
        )
        for a in range(4)
    ]
    return forces, stresses


def spread_row(spread, pitch, row, lanes, rels, wanted):
    one, zero = jnp.ones((), BF16), jnp.zeros((), BF16)
    lane_ids = iota((LANES, LANES), 0).astype(F32).astype(BF16)
    left, right = [], []
    for a in range(4):
        data = spread[pl.ds(a * 5 * pitch + row, 8, stride=pitch), :]
        high, low = split2(data)
        both = jnp.concatenate([high, low], axis=0).astype(BF16)
        rel = tiled_rows(rels[a : a + 1], 16)
        left.append(jnp.concatenate([jnp.where(rel == jnp.asarray(j, BF16), both, zero) for j in wanted], axis=0))
        lane = tiled_rows(lanes[a : a + 1], LANES)
        right.append(jnp.where(lane == lane_ids, one, zero))
    out = lax.dot_general(
        jnp.concatenate(left, axis=1), jnp.concatenate(right, axis=1), NT, preferred_element_type=F32
    )
    return [out[16 * j : 16 * j + 8] + out[16 * j + 8 : 16 * j + 16] for j in range(len(wanted))]


def element_kernel(
    velocity, before, after, connectivity, grads, area, thickness, yields, stress, returned,
    new_stress, own, ext, spread, acc,
):
    del returned
    nodes = velocity.shape[1]
    rows = nodes // LANES
    pitch = rows + 8
    chunk = 8 * LANES
    for c in range(5):
        at = FACE_ROWS + c
        ext[c * pitch : c * pitch + 1, :] = before[at : at + 1, :]
        ext[c * pitch + 1 : c * pitch + 2, :] = before[at + 5 : at + 6, :]
        for k in range(rows // 8):
            ext[c * pitch + 2 + 8 * k : c * pitch + 10 + 8 * k, :] = velocity[c, pl.ds(k * chunk, chunk)].reshape(8, LANES)
        ext[c * pitch + rows + 2 : c * pitch + rows + 3, :] = after[at : at + 1, :]
        ext[c * pitch + rows + 3 : c * pitch + rows + 4, :] = after[at + 5 : at + 6, :]
    spread[20 * pitch :, :] = jnp.zeros((3 * pitch, LANES), F32)

    def elements(k, carry):
        here = pl.ds(pl.multiple_of(k * chunk, chunk), chunk)
        first = pl.multiple_of(k * 8, 8)
        packed = pl.ds(first, 8)
        sources = [[ext[pl.ds(c * pitch + k * 8 + j + 1, 8), :] for j in range(3)] for c in range(5)]
        row_ids = iota((8, LANES), 0) + k * 8
        places = []
        for a in range(4):
            index = connectivity[a, here].reshape(8, LANES)
            places.append((index & (LANES - 1), (index >> 7) - row_ids))
        gx = [grads[0, a, here].reshape(8, LANES) for a in range(4)]
        gy = [grads[1, a, here].reshape(8, LANES) for a in range(4)]
        forces, stresses = element_pack(
            sources, places, gx, gy, thickness[packed, :], yields[packed, :], area[packed, :],
            lambda layer: [stress[layer, c, here].reshape(8, LANES) for c in range(5)],
        )
        for layer in range(5):
            for c in range(5):
                new_stress[layer, c, here] = stresses[layer][c].reshape(chunk)
        for a in range(4):
            for c in range(5):
                spread[pl.ds((a * 5 + c) * pitch + first, 8), :] = forces[a][c]
        return carry

    lax.fori_loop(0, rows // 8, elements, 0)
    blank = jnp.zeros((6, LANES), F32)

    def edge(n):
        at = FACE_ROWS + 10 + n
        return jnp.concatenate([before[at : at + 1, :], after[at : at + 1, :], blank], axis=0)

    sub = iota((8, LANES), 0)
    sources = [
        [
            jnp.concatenate(
                [ext[c * pitch + j : c * pitch + j + 1, :], ext[c * pitch + rows + 1 + j : c * pitch + rows + 2 + j, :], blank],
                axis=0,
            )
            for j in range(3)
        ]
        for c in range(5)
    ]
    places = []
    for a in range(4):
        index = edge(33 + a).astype(jnp.int32) + jnp.where(sub == 0, -nodes, nodes)
        places.append((index & (LANES - 1), jnp.where(sub == 0, (index >> 7) + 1, (index >> 7) - rows)))
    limit = edge(39)
    forces, _ = element_pack(
        sources, places, [edge(25 + a) for a in range(4)], [edge(29 + a) for a in range(4)],
        edge(38), jnp.where(limit > 0.0, limit, 1.0), edge(37),
        lambda layer: [edge(layer * 5 + c) for c in range(5)],
    )
    for a in range(4):
        for c in range(5):
            at = (a * 5 + c) * pitch + rows
            spread[at : at + 8, :] = forces[a][c]

    acc[...] = jnp.zeros_like(acc)

    def scatter(step, carry):
        b = step * 16
        parts = []
        for i in range(16):
            index = connectivity[:, pl.ds(pl.multiple_of((b + i) * LANES, LANES), LANES)]
            lanes = (index & (LANES - 1)).astype(F32)
            rels = ((index >> 7) - (b + i)).astype(F32)
            parts.append(spread_row(spread, pitch, b + i, lanes, rels, (0, 1, 2)))
        total = {}
        for i in range(16):
            for j in range(3):
                total[i + j] = parts[i][j] if i + j not in total else total[i + j] + parts[i][j]
        for n in range(18):
            at = pl.ds(pl.multiple_of((b + n) * 8, 8), 8)
            if n < 2:
                acc[at, :] += total[n]
            else:
                acc[at, :] = total[n]
        return carry

    lax.fori_loop(0, rows // 16, scatter, 0)
    for side, row, j in ((0, 1, 2), (1, rows, 0)):
        lanes = jnp.concatenate([place[0][side : side + 1] for place in places], axis=0).astype(F32)
        rels = jnp.concatenate([place[1][side : side + 1] for place in places], axis=0).astype(F32)
        acc[8 * row : 8 * row + 8, :] += spread_row(spread, pitch, rows + side, lanes, rels, (j,))[0]
    own[...] = acc[8 : 8 + 8 * rows, :]


def prepare_kernel(own, before, after, face, raw):
    own_rows = own.shape[0]
    face_tiles = (own_rows + 32) // 8
    raw[0:16, :] = before[0:FACE_ROWS, :]
    raw[16 : 16 + own_rows, :] = own[...]
    raw[16 + own_rows :, :] = after[0:FACE_ROWS, :]
    sub = iota((8, LANES), 0)

    def prepare(f):
        data = raw[pl.ds(pl.multiple_of(f * 8, 8), 8), :]
        centre = data - 0.5
        normal = [jnp.broadcast_to(data[3 + c : 4 + c], (8, LANES)) for c in range(3)]
        place = [jnp.broadcast_to(centre[c : c + 1], (8, LANES)) for c in range(3)]
        stiff = jnp.broadcast_to(data[6:7], (8, LANES))
        m_low = jnp.where(sub == 0, normal[0], jnp.where(sub == 1, normal[1], jnp.where(sub == 2, normal[2], 0.0)))
        coef_e = jnp.where(sub < 3, (2.0 / REACH_SQ * LOG2E) * centre, jnp.where(sub == 6, 1.0, 0.0))
        coef_d = -m_low
        inside = (sub >= 3) & (sub < 6)
        coef_a = jnp.where(inside, (-DAMPING) * stiff * data, jnp.where(sub == 7, stiff, 0.0))
        square = place[0] * place[0] + place[1] * place[1] + place[2] * place[2]
        along = normal[0] * place[0] + normal[1] * place[1] + normal[2] * place[2]
        zero = jnp.zeros((8, LANES), F32)
        pieces = []
        for coef, const in ((coef_e, (-LOG2E / REACH_SQ) * square), (coef_d, along), (coef_a, None)):
            high, low = split2(coef)
            last = zero
            if const is not None:
                c_high, c_low = split2(const)
                last = jnp.where(sub == 0, c_high, jnp.where(sub == 1, c_low, 0.0))
            pieces += [high, high, low, last]
        pieces.append(jnp.where(sub < 3, split2(m_low)[0], jnp.where(inside, split2(data)[1], 0.0)))
        turned = jnp.concatenate(pieces + [zero] * 3, axis=0).T
        face[pl.ds(pl.multiple_of(f * LANES, LANES), LANES), :] = turned.astype(BF16)

    def prepare_group(i, carry):
        for n in range(4):
            prepare(i * 4 + n)
        return carry

    lax.fori_loop(0, face_tiles // 4, prepare_group, 0)


def contact_kernel(pair_node, pair_face, pair_count, nodes, face, out, mean, table, acc, *, devices, tiles):
    row_ids, column_ids = iota((LANES, 3 * LANES), 0), iota((LANES, 3 * LANES), 1) // LANES
    picks = jnp.where((row_ids == 96 + column_ids) | (row_ids == 99 + column_ids), 1.0, 0.0).astype(BF16)
    step_rows = face.shape[0] // 2

    def widen(i, carry):
        at = pl.ds(pl.multiple_of(i * step_rows, step_rows), step_rows)
        mean[at, :] = lax.dot_general(face[at, :], picks, NN, preferred_element_type=F32)
        return carry

    lax.fori_loop(0, face.shape[0] // step_rows, widen, 0)
    total = devices * tiles
    acc[...] = jnp.zeros_like(acc)
    for c in range(6):
        flat = nodes[:, c * tiles : (c + 1) * tiles, :].reshape(total, LANES)
        if c == 0:
            table[pl.ds(7, total, stride=8), :] = jnp.where(flat > 0.5, 1.0, 0.0)
        flat = flat - (1.5, 0.5, 0.5)[c] if c < 3 else flat
        if c < 3:
            square = flat * flat if c == 0 else square + flat * flat
        table[pl.ds(c, total, stride=8), :] = flat
    table[pl.ds(6, total, stride=8), :] = (-LOG2E / REACH_SQ) * square
    ones = jnp.where(iota((8, LANES), 0) < 2, 1.0, 0.0)
    gap = jnp.zeros((32, LANES), BF16)

    def pair_force(node, which):
        high, low = split2(table[pl.ds(pl.multiple_of(node * 8, 8), 8), :])
        matrix = jnp.concatenate([high, low, high, ones], axis=0).astype(BF16)
        blocks = [jnp.concatenate([gap] * q + [matrix] + [gap] * (3 - q), axis=0) for q in range(3)]
        at = pl.ds(pl.multiple_of(which * LANES, LANES), LANES)
        terms = lax.dot_general(face[at, :], jnp.concatenate(blocks, axis=1), NN, preferred_element_type=F32)
        sums = [None] * 3
        for j in range(8):
            power, depth, scale = [terms[j * 16 : j * 16 + 16, q * LANES : (q + 1) * LANES] for q in range(3)]
            magnitude = jnp.exp2(power) * jnp.maximum(depth, 0.0) * scale
            at = pl.ds(pl.multiple_of(which * LANES + j * 16, 16), 16)
            for c in range(3):
                term = magnitude * mean[at, c * LANES : (c + 1) * LANES]
                term = term[:8] + term[8:]
                sums[c] = term if j == 0 else sums[c] + term
        return sums

    count = pair_count[0]
    group = math.gcd(32, pair_node.shape[0])

    def step(i, carry):
        ids = [i * group + n for n in range(group)]
        at = [pair_node[q] for q in ids]
        found = [pair_force(at[n], pair_face[ids[n]]) for n in range(group)]
        for n in range(group):
            keep = jnp.where(ids[n] < count, 1.0, 0.0)
            for c in range(3):
                rows = pl.ds(pl.multiple_of(at[n] * 24 + c * 8, 8), 8)
                acc[rows, :] += found[n][c] * keep
        return carry

    lax.fori_loop(0, (count + group - 1) // group, step, 0)
    for c in range(3):
        value = acc[pl.ds(c * 8, total, stride=24), :]
        for r in range(1, 8):
            value = value + acc[pl.ds(c * 8 + r, total, stride=24), :]
        out[:, c * tiles : (c + 1) * tiles, :] = value.reshape(devices, tiles, LANES)


def final_kernel(back, slot, own, velocity, inv_mass, out, table, *, tiles):
    devices = back.shape[0]
    rows = slot.shape[0]
    for c in range(3):
        square = back[:, c * tiles : (c + 1) * tiles, :].reshape(devices * tiles, LANES).T
        for half, data in enumerate((square[:LOW], square[LOW:])):
            high, low = split2(data)
            table[half, 2 * c * LOW : (2 * c + 1) * LOW, :] = high.astype(BF16)
            table[half, (2 * c + 1) * LOW : (2 * c + 2) * LOW, :] = low.astype(BF16)
    group_ids = iota((2 * LANES, LANES), 0).astype(F32).astype(BF16)
    low_ids = iota((LOW, LANES), 0)
    one, zero = jnp.ones((), BF16), jnp.zeros((), BF16)
    sub = iota((8, LANES), 0)

    def step(k, carry):
        slots = slot[pl.ds(pl.multiple_of(k * 64, 64), 64), :]
        low = slots & (LOW - 1)
        group = (((slots >> 6) & 1) * LANES + (slots >> 7)).astype(F32)
        hot = [jnp.where(tiled_rows(group[i : i + 1], 2 * LANES) == group_ids, one, zero) for i in range(64)]
        left = jnp.concatenate([table[0], table[1]], axis=1)
        picked = lax.dot_general(left, jnp.concatenate(hot, axis=1), NN, preferred_element_type=F32)
        for i in range(64):
            r = k * 64 + i
            mask = jnp.broadcast_to(low[i : i + 1], (LOW, LANES)) == low_ids
            contact = jnp.zeros((8, LANES), F32)
            for c in range(3):
                part = picked[2 * c * LOW : (2 * c + 2) * LOW, i * LANES : (i + 1) * LANES]
                value = jnp.sum(jnp.where(mask, part[:LOW] + part[LOW:], 0.0), axis=0, keepdims=True)
                contact = jnp.where(sub == c, value, contact)
            lanes = pl.ds(pl.multiple_of(r * LANES, LANES), LANES)
            total = contact - own[pl.ds(pl.multiple_of(r * 8, 8), 8), :]
            out[:, lanes] = velocity[:, lanes] + inv_mass[pl.ds(r, 1), :] * total[0:5]
        return carry

    lax.fori_loop(0, rows // 64, step, 0)


def call(kernel, outs, ins, scratch, cost, smem=0, limit=12, away=(), out_away=()):
    vmem = pl.BlockSpec(memory_space=pltpu.VMEM)
    scalar = pl.BlockSpec(memory_space=pltpu.SMEM)
    return pl.pallas_call(
        kernel,
        out_shape=outs,
        in_specs=[scalar if n < smem else pl.BlockSpec(memory_space=pltpu.HBM) if n in away else vmem for n in range(len(ins))],
        out_specs=tuple(pl.BlockSpec(memory_space=pl.ANY) if n in out_away else vmem for n in range(len(outs)))
        if isinstance(outs, tuple)
        else vmem,
        scratch_shapes=scratch,
        compiler_params=pltpu.CompilerParams(vmem_limit_bytes=limit << 20),
        cost_estimate=pl.CostEstimate(flops=cost, bytes_accessed=cost // 100, transcendentals=0),
    )(*ins)


def body(
    velocity, position, inv_mass, connectivity, shape_grad, area, thickness, yield_stress, stress,
    contact_owner, face_center, face_angle, face_stiffness, ghost_list, pair_node, pair_face, pair_count,
):
    axes = ("dom", "sub")
    devices = lax.axis_size("dom") * lax.axis_size("sub")
    nodes = velocity.shape[1]
    faces = face_center.shape[1]
    rows = nodes // LANES
    capacity = 2 * nodes // devices
    tiles = capacity // LANES
    shape = lambda *s: jax.ShapeDtypeStruct(s, F32)
    view = lambda x: x.reshape(-1, LANES)

    outgoing, slot = call(
        functools.partial(arrange_kernel, devices=devices, capacity=capacity),
        (shape(devices, 6 * tiles, LANES), jax.ShapeDtypeStruct((rows, LANES), jnp.int32)),
        (view(contact_owner), position, velocity),
        [
            pltpu.VMEM((12 * THIN, 2 * LANES), F32),
            pltpu.VMEM((8 * (rows + 1), LANES), F32),
            pltpu.VMEM((8, LANES), jnp.int32),
            pltpu.SMEM((8, LANES), jnp.int32),
            pltpu.VMEM(position.shape, F32),
            pltpu.VMEM(velocity.shape, F32),
            pltpu.SemaphoreType.DMA((3,)),
        ],
        10**9,
        limit=56,
        away=(1, 2),
    )
    incoming = lax.all_to_all(outgoing, axes, split_axis=0, concat_axis=0, tiled=True)
    own_faces, send_up, send_down = call(
        packet_kernel,
        (shape(faces // LANES * 8, LANES), shape(PACKET, LANES), shape(PACKET, LANES)),
        (
            face_center, face_angle, view(face_stiffness), view(ghost_list), velocity, stress, shape_grad,
            connectivity, view(area), view(thickness), view(yield_stress), slot,
        ),
        [
            pltpu.VMEM((2, 5, 2 * LANES), F32),
            pltpu.VMEM((2, 5, 5, LANES), F32),
            pltpu.VMEM((2, 2, 4, LANES), F32),
            pltpu.VMEM((2, 4, LANES), jnp.int32),
            pltpu.VMEM((2, 3, 1, LANES), F32),
            pltpu.SemaphoreType.DMA((14,)),
        ],
        10**8,
        away=range(4, 12),
    )
    up = [(i, i + 1) for i in range(devices - 1)]
    down = [(j, i) for i, j in up]
    before = lax.ppermute(send_up, axes, up)
    after = lax.ppermute(send_down, axes, down)
    face_rows = own_faces.shape[0] + 32
    face_matrix = call(
        prepare_kernel,
        jax.ShapeDtypeStruct((face_rows * 16, LANES), BF16),
        (own_faces, before, after),
        [pltpu.VMEM((face_rows, LANES), F32)],
        10**8,
    )
    returned = call(
        functools.partial(contact_kernel, devices=devices, tiles=tiles),
        shape(devices, 3 * tiles, LANES),
        (pair_node, pair_face, pair_count, incoming, face_matrix),
        [
            pltpu.VMEM((face_rows * 16, 3 * LANES), F32),
            pltpu.VMEM((devices * tiles * 8, LANES), F32),
            pltpu.VMEM((devices * tiles * 24, LANES), F32),
        ],
        10**9,
        smem=3,
    )
    back = lax.all_to_all(returned, axes, split_axis=0, concat_axis=0, tiled=True)
    new_stress, own = call(
        element_kernel,
        (shape(*stress.shape), shape(8 * rows, LANES)),
        (
            velocity, before, after, connectivity, shape_grad, view(area), view(thickness), view(yield_stress),
            stress, returned,
        ),
        [
            pltpu.VMEM((5 * (rows + 8), LANES), F32),
            pltpu.VMEM((23 * (rows + 8), LANES), F32),
            pltpu.VMEM((8 * (rows + 2), LANES), F32),
        ],
        10**9,
        away=(9,),
    )
    new_velocity = call(
        functools.partial(final_kernel, tiles=tiles),
        shape(*velocity.shape),
        (back, slot, own, velocity, view(inv_mass)),
        [pltpu.VMEM((2, 6 * LOW, LANES), BF16)],
        10**9,
    )
    return (new_velocity, new_stress)


def solution(mesh):
    split = ("dom", "sub")
    in_specs = (
        P(None, split), P(None, split), P(split), P(None, split), P(None, None, split),
        P(split), P(split), P(split), P(None, None, split), P(split, None),
        P(None, split), P(None, split), P(split), P(split), P(split), P(split), P(split),
    )
    out_specs = (P(None, split), P(None, None, split))
    return jax.shard_map(body, mesh=mesh, in_specs=in_specs, out_specs=out_specs, check_vma=False)
```

```python
import functools
import math

import jax
import jax.numpy as jnp
from jax import lax
from jax.experimental import pallas as pl
from jax.experimental.pallas import tpu as pltpu
from jax.sharding import PartitionSpec as P

LANES = 128
LOW = 64
THIN = 32

LOBATTO_POINTS = (-1.0, -0.6546536707079771, 0.0, 0.6546536707079771, 1.0)
LOBATTO_WEIGHTS = (0.1, 49.0 / 90.0, 32.0 / 45.0, 49.0 / 90.0, 0.1)
PLANE_MODULUS = 1.0 / 0.91
POISSON = 0.3
SHEAR_MODULUS = 5.0 / 6.0 / 2.6
DAMPING = 0.3
REACH_SQ = 0.5
LOG2E = 1.4426950408889634

F32 = jnp.float32
BF16 = jnp.bfloat16
NT = (((1,), (1,)), ((), ()))
NN = (((1,), (0,)), ((), ()))


def iota(shape, dim):
    return lax.broadcasted_iota(jnp.int32, shape, dim)


def split2(x):
    high = x.astype(BF16).astype(F32)
    return high, x - high


def tiled_rows(row, count):
    packed = jnp.broadcast_to(row, (16, row.shape[1])).astype(BF16)
    return packed if count == 16 else jnp.concatenate([packed] * (count // 16), axis=0)


def arrange_kernel(
    owner, position_away, velocity_away, out, slot_out, acc, ordered, bounds, bounds_scalar, position, velocity,
    arrived, *, devices, capacity
):
    rows = owner.shape[0]
    load_position = pltpu.make_async_copy(position_away, position, arrived.at[1])
    load_velocity = pltpu.make_async_copy(velocity_away, velocity, arrived.at[2])
    load_position.start()
    load_velocity.start()
    tiles = capacity // LANES
    upper = jnp.where(iota((LANES, 2 * LANES), 1) > iota((LANES, 2 * LANES), 0), 1.0, 0.0).astype(BF16)
    device_ids = iota((devices, LANES), 0)

    def count(k, base):
        owners = owner[pl.ds(pl.multiple_of(k * 32, 32), 32), :]
        masks = [jnp.broadcast_to(owners[s : s + 1], (devices, LANES)) == device_ids for s in range(32)]
        hot = jnp.concatenate([jnp.where(m, 1.0, 0.0).astype(BF16) for m in masks], axis=0)
        counted = lax.dot_general(hot, upper, NN, preferred_element_type=F32)
        ranks = []
        for s in range(32):
            part = counted[s * devices : (s + 1) * devices]
            ranks.append(jnp.sum(jnp.where(masks[s], part[:, :LANES] + base, 0.0), axis=0, keepdims=True))
            base = base + part[:, LANES:]
        rank = jnp.concatenate(ranks, axis=0).astype(jnp.int32)
        slot_out[pl.ds(pl.multiple_of(k * 32, 32), 32), :] = owners * capacity + rank
        return base

    totals = lax.fori_loop(0, rows // 32, count, jnp.zeros((devices, LANES), F32))
    lower = jnp.where(iota((devices, devices), 0) > iota((devices, devices), 1), 1.0, 0.0).astype(BF16)
    high, low = split2(totals)
    starts = lax.dot_general(lower, jnp.concatenate([high, low], axis=1).astype(BF16), NN, preferred_element_type=F32)
    starts = starts[:, :LANES] + starts[:, LANES:]
    by_lane = []
    for data in (starts, totals):
        if devices < LANES:
            data = jnp.concatenate([data, jnp.zeros((LANES - devices, LANES), F32)], axis=0)
        by_lane.append(data.T[0:8].astype(jnp.int32))
    start_lanes = by_lane[0]
    bounds[...] = jnp.where(iota((8, LANES), 0) == 0, by_lane[0], by_lane[1])
    copy = pltpu.make_async_copy(bounds, bounds_scalar, arrived.at[0])
    copy.start()

    low_ids = iota((THIN, LANES), 0).astype(F32).astype(BF16)
    group_ids = iota((2 * LANES, LANES), 0).astype(F32).astype(BF16)
    acc[...] = jnp.zeros_like(acc)
    one, zero = jnp.ones((), BF16), jnp.zeros((), BF16)
    load_position.wait()
    load_velocity.wait()

    def sort(k, carry):
        owners = owner[pl.ds(pl.multiple_of(k * 64, 64), 64), :]
        rank = slot_out[pl.ds(pl.multiple_of(k * 64, 64), 64), :] - owners * capacity
        place = jnp.concatenate([jnp.take_along_axis(start_lanes, owners[8 * h : 8 * h + 8], axis=1) for h in range(8)], axis=0) + rank
        low = (place & (THIN - 1)).astype(F32)
        group = (((place >> 6) & 1) * LANES + ((place >> 5) & 1) * (LANES // 2) + (place >> 7)).astype(F32)
        left, right = [], []
        for s in range(64):
            lanes = pl.ds(pl.multiple_of(k * 64 * LANES + s * LANES, LANES), LANES)
            hot_low = jnp.where(tiled_rows(low[s : s + 1], THIN) == low_ids, one, zero)
            right.append(jnp.where(tiled_rows(group[s : s + 1], 2 * LANES) == group_ids, one, zero))
            where = position[:, lanes]
            where = where + jnp.where(iota(where.shape, 0) == 0, 1.0, 0.0)
            column = []
            for data in (where, velocity[0:3, lanes]):
                parts = split2(data)
                for c in range(3):
                    for half in range(2):
                        column.append(hot_low * tiled_rows(parts[half][c : c + 1], THIN))
            left.append(jnp.concatenate(column, axis=0))
        acc[...] += lax.dot_general(
            jnp.concatenate(left, axis=1), jnp.concatenate(right, axis=1), NT, preferred_element_type=F32
        )
        return carry

    lax.fori_loop(0, rows // 64, sort, 0)
    for c in range(6):
        both = acc[2 * c * THIN : (2 * c + 1) * THIN, :] + acc[(2 * c + 1) * THIN : (2 * c + 2) * THIN, :]
        pieces = []
        for data in (both[:, :LANES], both[:, LANES:]):
            pieces += [data, pltpu.roll(data, LANES // 2, 1)]
        ordered[pl.ds(c, rows, stride=8), :] = jnp.concatenate(pieces, axis=0).T[0:rows]
    ordered[8 * rows :, :] = jnp.zeros((8, LANES), F32)
    copy.wait()
    lane = iota((8, LANES), 1)

    def place_runs(i, carry):
        for n in range(8):
            device = i * 8 + n
            start, amount = bounds_scalar[0, device], bounds_scalar[1, device]
            for t in range(tiles):
                at = start + t * LANES
                row = jnp.minimum(at >> 7, rows - 1)
                shift = at & (LANES - 1)
                this = ordered[pl.ds(pl.multiple_of(row * 8, 8), 8), :]
                following = ordered[pl.ds(pl.multiple_of(row * 8 + 8, 8), 8), :]
                turned = pltpu.roll(jnp.where(lane >= shift, this, following), (LANES - shift) & (LANES - 1), 1)
                out[device, pl.ds(t, 6, stride=tiles), :] = jnp.where(lane < amount - t * LANES, turned, 0.0)[0:6]
        return carry

    lax.fori_loop(0, devices // 8, place_runs, 0)


FACE_ROWS = 16
PACKET = 72


def packet_kernel(
    center, angle, stiffness, ghost, velocity, stress, grads, connectivity, area, thickness, yields, slot,
    own, up, down, edge_velocity, edge_stress, edge_grads, edge_nodes, edge_scalars, arrived,
):
    del slot
    nodes = velocity.shape[1]
    rows = nodes // LANES
    copies = []
    for side in range(2):
        wide = pl.ds(0, 2 * LANES) if side else pl.ds(nodes - 2 * LANES, 2 * LANES)
        last = pl.ds(0, LANES) if side else pl.ds(nodes - LANES, LANES)
        row = pl.ds(0, 1) if side else pl.ds(rows - 1, 1)
        pairs = [
            (velocity.at[:, wide], edge_velocity.at[side]),
            (stress.at[:, :, last], edge_stress.at[side]),
            (grads.at[:, :, last], edge_grads.at[side]),
            (connectivity.at[:, last], edge_nodes.at[side]),
            (area.at[row], edge_scalars.at[side, 0]),
            (thickness.at[row], edge_scalars.at[side, 1]),
            (yields.at[row], edge_scalars.at[side, 2]),
        ]
        for n, (source, target) in enumerate(pairs):
            copies.append(pltpu.make_async_copy(source, target, arrived.at[side * len(pairs) + n]))
    for copy in copies:
        copy.start()
    count = stiffness.shape[0]
    azimuth = angle[0, :].reshape(count, LANES)
    elevation = angle[1, :].reshape(count, LANES)
    flat = jnp.cos(elevation)
    data = [center[c, :].reshape(count, LANES) for c in range(3)]
    data += [jnp.cos(azimuth) * flat, jnp.sin(azimuth) * flat, jnp.sin(elevation), stiffness[...]]
    wanted = ghost[...]
    wanted = jnp.concatenate([wanted, wanted], axis=0)
    row_of, lane_of = wanted >> 7, wanted & (LANES - 1)
    up[...] = jnp.zeros_like(up)
    down[...] = jnp.zeros_like(down)
    own[pl.ds(7, count, stride=8), :] = jnp.zeros((count, LANES), F32)
    for c in range(7):
        own[pl.ds(c, count, stride=8), :] = data[c]
        found = jnp.zeros((8, LANES), F32)
        for r in range(count):
            source = jnp.broadcast_to(data[c][r : r + 1], (8, LANES))
            found = jnp.where(row_of == r, jnp.take_along_axis(source, lane_of, axis=1), found)
        for t in range(2):
            down[8 * t + c : 8 * t + c + 1, :] = found[t : t + 1]
            up[8 * t + c : 8 * t + c + 1, :] = found[2 + t : 3 + t]
    for copy in copies:
        copy.wait()
    for side, out in ((0, up), (1, down)):
        at = FACE_ROWS
        out[at : at + 5, :] = edge_velocity[side, :, :LANES]
        out[at + 5 : at + 10, :] = edge_velocity[side, :, LANES:]
        at += 10
        for layer in range(5):
            out[at : at + 5, :] = edge_stress[side, layer]
            at += 5
        for g in range(2):
            out[at : at + 4, :] = edge_grads[side, g]
            at += 4
        out[at : at + 4, :] = edge_nodes[side].astype(F32)
        at += 4
        for n in range(3):
            out[at + n : at + n + 1, :] = edge_scalars[side, n]


def element_pack(sources, places, gx, gy, thick, limit, area, old_stress):
    corner = []
    for lane, rel in places:
        second, third = rel == 1, rel == 2
        values = []
        for c in range(5):
            g = [jnp.take_along_axis(sources[c][j], lane, axis=1) for j in range(3)]
            values.append(jnp.where(third, g[2], jnp.where(second, g[1], g[0])))
        corner.append(values)

    def total(f):
        t = [f(a) for a in range(4)]
        return (t[0] + t[1]) + (t[2] + t[3])

    memb_xx = total(lambda a: gx[a] * corner[a][0])
    bend_xx = total(lambda a: gx[a] * corner[a][4])
    memb_yy = total(lambda a: gy[a] * corner[a][1])
    bend_yy = -total(lambda a: gy[a] * corner[a][3])
    memb_xy = total(lambda a: gy[a] * corner[a][0] + gx[a] * corner[a][1])
    bend_xy = total(lambda a: gy[a] * corner[a][4] - gx[a] * corner[a][3])
    shear_xz = total(lambda a: gx[a] * corner[a][2]) + 0.25 * total(lambda a: corner[a][4])
    shear_yz = total(lambda a: gy[a] * corner[a][2]) - 0.25 * total(lambda a: corner[a][3])
    half_area = 0.5 * thick * area
    force = [None] * 5
    moment = [None] * 3
    stresses = []
    for layer in range(5):
        height = (0.5 * LOBATTO_POINTS[layer]) * thick
        xx = memb_xx + height * bend_xx
        yy = memb_yy + height * bend_yy
        xy = memb_xy + height * bend_xy
        old = old_stress(layer)
        t = [
            old[0] + PLANE_MODULUS * (xx + POISSON * yy),
            old[1] + PLANE_MODULUS * (yy + POISSON * xx),
            old[2] + (PLANE_MODULUS * 0.5 * (1.0 - POISSON)) * xy,
            old[3] + SHEAR_MODULUS * shear_xz,
            old[4] + SHEAR_MODULUS * shear_yz,
        ]
        plus, minus = t[0] + t[1], t[0] - t[1]
        mises = jnp.sqrt(
            0.25 * (plus * plus) + 0.75 * (minus * minus) + 3.0 * (t[2] * t[2] + t[3] * t[3] + t[4] * t[4])
        )
        factor = limit / jnp.maximum(mises, limit)
        weight = LOBATTO_WEIGHTS[layer] * half_area
        lever = weight * height
        values = [t[c] * factor for c in range(5)]
        stresses.append(values)
        for c in range(5):
            term = weight * values[c]
            force[c] = term if layer == 0 else force[c] + term
            if c < 3 and layer != 2:
                term = lever * values[c]
                moment[c] = term if layer == 0 else moment[c] + term
    forces = [
        (
            gx[a] * force[0] + gy[a] * force[2],
            gy[a] * force[1] + gx[a] * force[2],
            gx[a] * force[3] + gy[a] * force[4],
            -(gy[a] * moment[1] + gx[a] * moment[2]) - 0.25 * force[4],
            gx[a] * moment[0] + gy[a] * moment[2] + 0.25 * force[3],
        )
        for a in range(4)
    ]
    return forces, stresses


def spread_row(spread, pitch, row, lanes, rels, wanted):
    one, zero = jnp.ones((), BF16), jnp.zeros((), BF16)
    lane_ids = iota((LANES, LANES), 0).astype(F32).astype(BF16)
    left, right = [], []
    for a in range(4):
        data = spread[pl.ds(a * 5 * pitch + row, 8, stride=pitch), :]
        high, low = split2(data)
        both = jnp.concatenate([high, low], axis=0).astype(BF16)
        rel = tiled_rows(rels[a : a + 1], 16)
        left.append(jnp.concatenate([jnp.where(rel == jnp.asarray(j, BF16), both, zero) for j in wanted], axis=0))
        lane = tiled_rows(lanes[a : a + 1], LANES)
        right.append(jnp.where(lane == lane_ids, one, zero))
    out = lax.dot_general(
        jnp.concatenate(left, axis=1), jnp.concatenate(right, axis=1), NT, preferred_element_type=F32
    )
    return [out[16 * j : 16 * j + 8] + out[16 * j + 8 : 16 * j + 16] for j in range(len(wanted))]


def element_kernel(
    velocity, before, after, connectivity, grads, area, thickness, yields, stress, returned,
    new_stress, own, ext, spread, acc,
):
    del returned
    nodes = velocity.shape[1]
    rows = nodes // LANES
    pitch = rows + 8
    chunk = 8 * LANES
    for c in range(5):
        at = FACE_ROWS + c
        ext[c * pitch : c * pitch + 1, :] = before[at : at + 1, :]
        ext[c * pitch + 1 : c * pitch + 2, :] = before[at + 5 : at + 6, :]
        for k in range(rows // 8):
            ext[c * pitch + 2 + 8 * k : c * pitch + 10 + 8 * k, :] = velocity[c, pl.ds(k * chunk, chunk)].reshape(8, LANES)
        ext[c * pitch + rows + 2 : c * pitch + rows + 3, :] = after[at : at + 1, :]
        ext[c * pitch + rows + 3 : c * pitch + rows + 4, :] = after[at + 5 : at + 6, :]
    spread[20 * pitch :, :] = jnp.zeros((3 * pitch, LANES), F32)

    def elements(k, carry):
        here = pl.ds(pl.multiple_of(k * chunk, chunk), chunk)
        first = pl.multiple_of(k * 8, 8)
        packed = pl.ds(first, 8)
        sources = [[ext[pl.ds(c * pitch + k * 8 + j + 1, 8), :] for j in range(3)] for c in range(5)]
        row_ids = iota((8, LANES), 0) + k * 8
        places = []
        for a in range(4):
            index = connectivity[a, here].reshape(8, LANES)
            places.append((index & (LANES - 1), (index >> 7) - row_ids))
        gx = [grads[0, a, here].reshape(8, LANES) for a in range(4)]
        gy = [grads[1, a, here].reshape(8, LANES) for a in range(4)]
        forces, stresses = element_pack(
            sources, places, gx, gy, thickness[packed, :], yields[packed, :], area[packed, :],
            lambda layer: [stress[layer, c, here].reshape(8, LANES) for c in range(5)],
        )
        for layer in range(5):
            for c in range(5):
                new_stress[layer, c, here] = stresses[layer][c].reshape(chunk)
        for a in range(4):
            for c in range(5):
                spread[pl.ds((a * 5 + c) * pitch + first, 8), :] = forces[a][c]
        return carry

    lax.fori_loop(0, rows // 8, elements, 0)
    blank = jnp.zeros((6, LANES), F32)

    def edge(n):
        at = FACE_ROWS + 10 + n
        return jnp.concatenate([before[at : at + 1, :], after[at : at + 1, :], blank], axis=0)

    sub = iota((8, LANES), 0)
    sources = [
        [
            jnp.concatenate(
                [ext[c * pitch + j : c * pitch + j + 1, :], ext[c * pitch + rows + 1 + j : c * pitch + rows + 2 + j, :], blank],
                axis=0,
            )
            for j in range(3)
        ]
        for c in range(5)
    ]
    places = []
    for a in range(4):
        index = edge(33 + a).astype(jnp.int32) + jnp.where(sub == 0, -nodes, nodes)
        places.append((index & (LANES - 1), jnp.where(sub == 0, (index >> 7) + 1, (index >> 7) - rows)))
    limit = edge(39)
    forces, _ = element_pack(
        sources, places, [edge(25 + a) for a in range(4)], [edge(29 + a) for a in range(4)],
        edge(38), jnp.where(limit > 0.0, limit, 1.0), edge(37),
        lambda layer: [edge(layer * 5 + c) for c in range(5)],
    )
    for a in range(4):
        for c in range(5):
            at = (a * 5 + c) * pitch + rows
            spread[at : at + 8, :] = forces[a][c]

    acc[...] = jnp.zeros_like(acc)

    def scatter(step, carry):
        b = step * 16
        parts = []
        for i in range(16):
            index = connectivity[:, pl.ds(pl.multiple_of((b + i) * LANES, LANES), LANES)]
            lanes = (index & (LANES - 1)).astype(F32)
            rels = ((index >> 7) - (b + i)).astype(F32)
            parts.append(spread_row(spread, pitch, b + i, lanes, rels, (0, 1, 2)))
        total = {}
        for i in range(16):
            for j in range(3):
                total[i + j] = parts[i][j] if i + j not in total else total[i + j] + parts[i][j]
        for n in range(18):
            at = pl.ds(pl.multiple_of((b + n) * 8, 8), 8)
            if n < 2:
                acc[at, :] += total[n]
            else:
                acc[at, :] = total[n]
        return carry

    lax.fori_loop(0, rows // 16, scatter, 0)
    for side, row, j in ((0, 1, 2), (1, rows, 0)):
        lanes = jnp.concatenate([place[0][side : side + 1] for place in places], axis=0).astype(F32)
        rels = jnp.concatenate([place[1][side : side + 1] for place in places], axis=0).astype(F32)
        acc[8 * row : 8 * row + 8, :] += spread_row(spread, pitch, rows + side, lanes, rels, (j,))[0]
    own[...] = acc[8 : 8 + 8 * rows, :]


def prepare_kernel(own, before, after, face, raw):
    own_rows = own.shape[0]
    face_tiles = (own_rows + 32) // 8
    raw[0:16, :] = before[0:FACE_ROWS, :]
    raw[16 : 16 + own_rows, :] = own[...]
    raw[16 + own_rows :, :] = after[0:FACE_ROWS, :]
    sub = iota((8, LANES), 0)

    def prepare(f):
        data = raw[pl.ds(pl.multiple_of(f * 8, 8), 8), :]
        centre = data - 0.5
        normal = [jnp.broadcast_to(data[3 + c : 4 + c], (8, LANES)) for c in range(3)]
        place = [jnp.broadcast_to(centre[c : c + 1], (8, LANES)) for c in range(3)]
        stiff = jnp.broadcast_to(data[6:7], (8, LANES))
        m_low = jnp.where(sub == 0, normal[0], jnp.where(sub == 1, normal[1], jnp.where(sub == 2, normal[2], 0.0)))
        coef_e = jnp.where(sub < 3, (2.0 / REACH_SQ * LOG2E) * centre, jnp.where(sub == 6, 1.0, 0.0))
        coef_d = -m_low
        inside = (sub >= 3) & (sub < 6)
        coef_a = jnp.where(inside, (-DAMPING) * stiff * data, jnp.where(sub == 7, stiff, 0.0))
        square = place[0] * place[0] + place[1] * place[1] + place[2] * place[2]
        along = normal[0] * place[0] + normal[1] * place[1] + normal[2] * place[2]
        zero = jnp.zeros((8, LANES), F32)
        pieces = []
        for coef, const in ((coef_e, (-LOG2E / REACH_SQ) * square), (coef_d, along), (coef_a, None)):
            high, low = split2(coef)
            last = zero
            if const is not None:
                c_high, c_low = split2(const)
                last = jnp.where(sub == 0, c_high, jnp.where(sub == 1, c_low, 0.0))
            pieces += [high, high, low, last]
        pieces.append(jnp.where(sub < 3, split2(m_low)[0], jnp.where(inside, split2(data)[1], 0.0)))
        turned = jnp.concatenate(pieces + [zero] * 3, axis=0).T
        face[pl.ds(pl.multiple_of(f * LANES, LANES), LANES), :] = turned.astype(BF16)

    def prepare_group(i, carry):
        for n in range(4):
            prepare(i * 4 + n)
        return carry

    lax.fori_loop(0, face_tiles // 4, prepare_group, 0)


def contact_kernel(pair_node, pair_face, pair_count, nodes, face, out, mean, table, acc, *, devices, tiles):
    row_ids, column_ids = iota((LANES, 3 * LANES), 0), iota((LANES, 3 * LANES), 1) // LANES
    picks = jnp.where((row_ids == 96 + column_ids) | (row_ids == 99 + column_ids), 1.0, 0.0).astype(BF16)
    step_rows = face.shape[0] // 2

    def widen(i, carry):
        at = pl.ds(pl.multiple_of(i * step_rows, step_rows), step_rows)
        mean[at, :] = lax.dot_general(face[at, :], picks, NN, preferred_element_type=F32)
        return carry

    lax.fori_loop(0, face.shape[0] // step_rows, widen, 0)
    total = devices * tiles
    acc[...] = jnp.zeros_like(acc)
    for c in range(6):
        flat = nodes[:, c * tiles : (c + 1) * tiles, :].reshape(total, LANES)
        if c == 0:
            table[pl.ds(7, total, stride=8), :] = jnp.where(flat > 0.5, 1.0, 0.0)
        flat = flat - (1.5, 0.5, 0.5)[c] if c < 3 else flat
        if c < 3:
            square = flat * flat if c == 0 else square + flat * flat
        table[pl.ds(c, total, stride=8), :] = flat
    table[pl.ds(6, total, stride=8), :] = (-LOG2E / REACH_SQ) * square
    ones = jnp.where(iota((8, LANES), 0) < 2, 1.0, 0.0)
    gap = jnp.zeros((32, LANES), BF16)

    def pair_force(node, which):
        high, low = split2(table[pl.ds(pl.multiple_of(node * 8, 8), 8), :])
        matrix = jnp.concatenate([high, low, high, ones], axis=0).astype(BF16)
        blocks = [jnp.concatenate([gap] * q + [matrix] + [gap] * (3 - q), axis=0) for q in range(3)]
        at = pl.ds(pl.multiple_of(which * LANES, LANES), LANES)
        terms = lax.dot_general(face[at, :], jnp.concatenate(blocks, axis=1), NN, preferred_element_type=F32)
        sums = [None] * 3
        for j in range(8):
            power, depth, scale = [terms[j * 16 : j * 16 + 16, q * LANES : (q + 1) * LANES] for q in range(3)]
            magnitude = jnp.exp2(power) * jnp.maximum(depth, 0.0) * scale
            at = pl.ds(pl.multiple_of(which * LANES + j * 16, 16), 16)
            for c in range(3):
                term = magnitude * mean[at, c * LANES : (c + 1) * LANES]
                term = term[:8] + term[8:]
                sums[c] = term if j == 0 else sums[c] + term
        return sums

    count = pair_count[0]
    group = math.gcd(64, pair_node.shape[0])

    def step(i, carry):
        ids = [i * group + n for n in range(group)]
        at = [pair_node[q] for q in ids]
        found = [pair_force(at[n], pair_face[ids[n]]) for n in range(group)]
        for n in range(group):
            keep = jnp.where(ids[n] < count, 1.0, 0.0)
            for c in range(3):
                rows = pl.ds(pl.multiple_of(at[n] * 24 + c * 8, 8), 8)
                acc[rows, :] += found[n][c] * keep
        return carry

    lax.fori_loop(0, (count + group - 1) // group, step, 0)
    for c in range(3):
        value = acc[pl.ds(c * 8, total, stride=24), :]
        for r in range(1, 8):
            value = value + acc[pl.ds(c * 8 + r, total, stride=24), :]
        out[:, c * tiles : (c + 1) * tiles, :] = value.reshape(devices, tiles, LANES)


def final_kernel(back, slot, own, velocity, inv_mass, out, table, *, tiles):
    devices = back.shape[0]
    rows = slot.shape[0]
    for c in range(3):
        square = back[:, c * tiles : (c + 1) * tiles, :].reshape(devices * tiles, LANES).T
        for half, data in enumerate((square[:LOW], square[LOW:])):
            high, low = split2(data)
            table[half, 2 * c * LOW : (2 * c + 1) * LOW, :] = high.astype(BF16)
            table[half, (2 * c + 1) * LOW : (2 * c + 2) * LOW, :] = low.astype(BF16)
    group_ids = iota((2 * LANES, LANES), 0).astype(F32).astype(BF16)
    low_ids = iota((LOW, LANES), 0)
    one, zero = jnp.ones((), BF16), jnp.zeros((), BF16)
    sub = iota((8, LANES), 0)

    def step(k, carry):
        slots = slot[pl.ds(pl.multiple_of(k * 64, 64), 64), :]
        low = slots & (LOW - 1)
        group = (((slots >> 6) & 1) * LANES + (slots >> 7)).astype(F32)
        hot = [jnp.where(tiled_rows(group[i : i + 1], 2 * LANES) == group_ids, one, zero) for i in range(64)]
        left = jnp.concatenate([table[0], table[1]], axis=1)
        picked = lax.dot_general(left, jnp.concatenate(hot, axis=1), NN, preferred_element_type=F32)
        for i in range(64):
            r = k * 64 + i
            mask = jnp.broadcast_to(low[i : i + 1], (LOW, LANES)) == low_ids
            contact = jnp.zeros((8, LANES), F32)
            for c in range(3):
                part = picked[2 * c * LOW : (2 * c + 2) * LOW, i * LANES : (i + 1) * LANES]
                value = jnp.sum(jnp.where(mask, part[:LOW] + part[LOW:], 0.0), axis=0, keepdims=True)
                contact = jnp.where(sub == c, value, contact)
            lanes = pl.ds(pl.multiple_of(r * LANES, LANES), LANES)
            total = contact - own[pl.ds(pl.multiple_of(r * 8, 8), 8), :]
            out[:, lanes] = velocity[:, lanes] + inv_mass[pl.ds(r, 1), :] * total[0:5]
        return carry

    lax.fori_loop(0, rows // 64, step, 0)


def call(kernel, outs, ins, scratch, cost, smem=0, limit=12, away=(), out_away=()):
    vmem = pl.BlockSpec(memory_space=pltpu.VMEM)
    scalar = pl.BlockSpec(memory_space=pltpu.SMEM)
    return pl.pallas_call(
        kernel,
        out_shape=outs,
        in_specs=[scalar if n < smem else pl.BlockSpec(memory_space=pltpu.HBM) if n in away else vmem for n in range(len(ins))],
        out_specs=tuple(pl.BlockSpec(memory_space=pl.ANY) if n in out_away else vmem for n in range(len(outs)))
        if isinstance(outs, tuple)
        else vmem,
        scratch_shapes=scratch,
        compiler_params=pltpu.CompilerParams(vmem_limit_bytes=limit << 20),
        cost_estimate=pl.CostEstimate(flops=cost, bytes_accessed=cost // 100, transcendentals=0),
    )(*ins)


def body(
    velocity, position, inv_mass, connectivity, shape_grad, area, thickness, yield_stress, stress,
    contact_owner, face_center, face_angle, face_stiffness, ghost_list, pair_node, pair_face, pair_count,
):
    axes = ("dom", "sub")
    devices = lax.axis_size("dom") * lax.axis_size("sub")
    nodes = velocity.shape[1]
    faces = face_center.shape[1]
    rows = nodes // LANES
    capacity = 2 * nodes // devices
    tiles = capacity // LANES
    shape = lambda *s: jax.ShapeDtypeStruct(s, F32)
    view = lambda x: x.reshape(-1, LANES)

    outgoing, slot = call(
        functools.partial(arrange_kernel, devices=devices, capacity=capacity),
        (shape(devices, 6 * tiles, LANES), jax.ShapeDtypeStruct((rows, LANES), jnp.int32)),
        (view(contact_owner), position, velocity),
        [
            pltpu.VMEM((12 * THIN, 2 * LANES), F32),
            pltpu.VMEM((8 * (rows + 1), LANES), F32),
            pltpu.VMEM((8, LANES), jnp.int32),
            pltpu.SMEM((8, LANES), jnp.int32),
            pltpu.VMEM(position.shape, F32),
            pltpu.VMEM(velocity.shape, F32),
            pltpu.SemaphoreType.DMA((3,)),
        ],
        10**9,
        limit=56,
        away=(1, 2),
    )
    incoming = lax.all_to_all(outgoing, axes, split_axis=0, concat_axis=0, tiled=True)
    own_faces, send_up, send_down = call(
        packet_kernel,
        (shape(faces // LANES * 8, LANES), shape(PACKET, LANES), shape(PACKET, LANES)),
        (
            face_center, face_angle, view(face_stiffness), view(ghost_list), velocity, stress, shape_grad,
            connectivity, view(area), view(thickness), view(yield_stress), slot,
        ),
        [
            pltpu.VMEM((2, 5, 2 * LANES), F32),
            pltpu.VMEM((2, 5, 5, LANES), F32),
            pltpu.VMEM((2, 2, 4, LANES), F32),
            pltpu.VMEM((2, 4, LANES), jnp.int32),
            pltpu.VMEM((2, 3, 1, LANES), F32),
            pltpu.SemaphoreType.DMA((14,)),
        ],
        10**8,
        away=range(4, 12),
    )
    up = [(i, i + 1) for i in range(devices - 1)]
    down = [(j, i) for i, j in up]
    before = lax.ppermute(send_up, axes, up)
    after = lax.ppermute(send_down, axes, down)
    face_rows = own_faces.shape[0] + 32
    face_matrix = call(
        prepare_kernel,
        jax.ShapeDtypeStruct((face_rows * 16, LANES), BF16),
        (own_faces, before, after),
        [pltpu.VMEM((face_rows, LANES), F32)],
        10**8,
    )
    returned = call(
        functools.partial(contact_kernel, devices=devices, tiles=tiles),
        shape(devices, 3 * tiles, LANES),
        (pair_node, pair_face, pair_count, incoming, face_matrix),
        [
            pltpu.VMEM((face_rows * 16, 3 * LANES), F32),
            pltpu.VMEM((devices * tiles * 8, LANES), F32),
            pltpu.VMEM((devices * tiles * 24, LANES), F32),
        ],
        10**9,
        smem=3,
    )
    back = lax.all_to_all(returned, axes, split_axis=0, concat_axis=0, tiled=True)
    new_stress, own = call(
        element_kernel,
        (shape(*stress.shape), shape(8 * rows, LANES)),
        (
            velocity, before, after, connectivity, shape_grad, view(area), view(thickness), view(yield_stress),
            stress, returned,
        ),
        [
            pltpu.VMEM((5 * (rows + 8), LANES), F32),
            pltpu.VMEM((23 * (rows + 8), LANES), F32),
            pltpu.VMEM((8 * (rows + 2), LANES), F32),
        ],
        10**9,
        away=(9,),
    )
    new_velocity = call(
        functools.partial(final_kernel, tiles=tiles),
        shape(*velocity.shape),
        (back, slot, own, velocity, view(inv_mass)),
        [pltpu.VMEM((2, 6 * LOW, LANES), BF16)],
        10**9,
    )
    return (new_velocity, new_stress)


def solution(mesh):
    split = ("dom", "sub")
    in_specs = (
        P(None, split), P(None, split), P(split), P(None, split), P(None, None, split),
        P(split), P(split), P(split), P(None, None, split), P(split, None),
        P(None, split), P(None, split), P(split), P(split), P(split), P(split), P(split),
    )
    out_specs = (P(None, split), P(None, None, split))
    return jax.shard_map(body, mesh=mesh, in_specs=in_specs, out_specs=out_specs, check_vma=False)
```
